512 devices in a mesh: roll: 64 (over x, z_hi, y, core), kv: 8 (over z_lo).
Axes of the slice: x: 4, y: 4, z: 16 (z_hi: 2, z_lo: 8; z = z_hi * 8 + z_lo), core: 2. Of those that a mesh axis runs over, the one named last changes fastest.
Arguments:
- queries: bfloat16 [64, 4, 2048], P('roll', None, 'kv'), may hold values from -8 to 8
- prompt_cache: bfloat16 [4, 16384, 1024], P(None, 'roll', 'kv'), may hold values from -4 to 4
- gen_cache: bfloat16 [64, 128, 1024], P('roll', None, 'kv'), may hold values from -4 to 4
- gen_lengths: int32 [64], P('roll'), may hold values from 1 to 128, 4096 in all
- new_kv: bfloat16 [64, 4, 1024], P('roll', None, 'kv'), may hold values from -4 to 4
- w_out: bfloat16 [2048, 2880], P('kv'), may hold values from -3 to 3
- residual: bfloat16 [64, 4, 2880], P('roll', None, 'kv'), may hold values from -10 to 10
- norm_gain: float32 [2880], P('kv'), may hold values from 0.5 to 1.5
- w_gate: bfloat16 [64, 2880, 1440], P('roll', None, 'kv'), may hold values from -0.109375 to 0.109375
- w_up: bfloat16 [64, 2880, 1440], P('roll', None, 'kv'), may hold values from -0.109375 to 0.109375
- w_down: bfloat16 [64, 1440, 2880], P('roll', 'kv'), may hold values from -0.15625 to 0.15625
- expert_ids: int32 [64, 4, 4], replicated, may hold values from 0 to 63, all different within a row; in each aligned block of 256 rows (0 to 255, 256 to 511, ..., all dimensions but the last counted through in order) at most 48 rows name the same one
- route_weights: float32 [64, 4, 4], replicated, may hold values from 0.05 to 0.5
Outputs:
- layer_out: bfloat16 [64, 4, 2880], P('roll', None, 'kv')
The draws below stay inside these ranges and needn't reach their ends.
Inputs may be any that keep to these rules, and one draw needn't show every extreme that they name: `expert_ids`: each row names 4 different experts; over all rows no expert is named more than 48 times, and one expert exactly 48 times. `gen_lengths`: the longest is exactly 128.
All inputs are finite; a program needn't handle non-finite values. No bound on the sum of `gen_lengths` on one device may be relied on, other than what follows from the above.
Results may differ from the reference program's by a relative error of at most 0.014.
Values may be sent and summed in bfloat16 or wider, within the bound.
A program may use at most 128 MiB of HBM per device.

```python
import math
import jax
import jax.numpy as jnp
import numpy as np
from jax import lax

D = 2880
HEAD = 64
QH = 32
KVH = 8
FFE = 1440
TOPK = 4
STEPS = 4
GROUP = 16
PLEN = 16384
GEN = 128
SAMPLES = 64
PROMPTS = 4
EXPERTS = 64
MOSTE = 48


def feature_profile():
    position = jnp.arange(D, dtype=jnp.float32) / (D - 1)
    return 0.25 * jnp.exp(position * jnp.log(9.0))


def draw_residual(key, part):
    noise_key = jax.random.fold_in(key, 41)
    shape = (SAMPLES, STEPS, D)
    values = jax.random.truncated_normal(noise_key, -4.0, 4.0, shape, jnp.float32)
    return (values * feature_profile()).astype(jnp.bfloat16)


def draw_w_out(key, part):
    noise_key = jax.random.fold_in(key, 53)
    shape = (QH * HEAD, D)
    values = 0.4 * jax.random.truncated_normal(noise_key, -2.5, 2.5, shape, jnp.float32)
    return (values * feature_profile()).astype(jnp.bfloat16)


def draw_queries(key, part):
    noise_key = jax.random.fold_in(key, 11)
    shape = (SAMPLES, STEPS, KVH, QH // KVH, HEAD)
    values = 2.0 * jax.random.truncated_normal(noise_key, -4.0, 4.0, shape, jnp.float32)
    return values.reshape(SAMPLES, STEPS, QH * HEAD).astype(jnp.bfloat16)


def draw_prompt_cache(key, part):
    noise_key = jax.random.fold_in(key, 23)
    shape = (PROMPTS, PLEN, KVH, 2, HEAD)
    values = jax.random.truncated_normal(noise_key, -4.0, 4.0, shape, jnp.float32)
    return values.reshape(PROMPTS, PLEN, KVH * 2 * HEAD).astype(jnp.bfloat16)


def levels(key, shape, split, low, high):
    def one(dim, shards_of):
        draws = jax.random.uniform(jax.random.fold_in(jax.random.fold_in(key, 6), dim), (shards_of,), jnp.float32, low / len(split), high / len(split))
        return jnp.repeat(jnp.exp(draws), shape[dim] // shards_of).reshape((-1,) + (1,) * (len(shape) - dim - 1))

    factor_of = one(*split[0])
    for cut in split[1:]:
        factor_of = factor_of * one(*cut)
    return factor_of


def split_up(count, total, bound, lean):
    loads = [(1 << 20) // math.isqrt(standing ** lean) + 1 for standing in range(2, count + 1)]
    spare, given = total - bound - (count - 1), [1] * (count - 1)
    while spare > 0:
        free = [i for i in range(count - 1) if given[i] < bound]
        pool, remaining = sum([loads[i] for i in free]), spare
        for i in free:
            addition = min(bound - given[i], max(1, remaining * loads[i] // pool), spare)
            given[i] = given[i] + addition
            spare = spare - addition
    return np.array([bound] + given)


def uneven_parts(stream_key, count, total, limit, slope):
    if count == 2:
        one = jax.random.randint(stream_key, (), max(1, total - limit), min(limit, total - 1) + 1)
        return jnp.stack([one, total - one])
    sizes = jnp.asarray(split_up(count, total, limit, slope), jnp.int32)
    twos = (count - 1) // 2
    donor, sink = sizes[1:1 + 2 * twos:2], sizes[2:2 + 2 * twos:2]
    margin = jnp.minimum(donor - 1, limit - sink)
    moved = jax.random.randint(jax.random.fold_in(stream_key, 1), (twos,), 0, 1 << 20) % (margin + 1)
    sizes = sizes.at[1:1 + 2 * twos:2].set(donor - moved).at[2:2 + 2 * twos:2].set(sink + moved)
    return sizes[jax.random.permutation(jax.random.fold_in(stream_key, 2), count)]


def routed_block(key, own, number, rows, number_of, top, reach, slope):
    ranking = jax.random.permutation(key, number_of)
    heavy_load, ordinary = load_shares(number_of, rows * top, reach, slope, True), load_shares(number_of, rows * top, reach, slope, False)
    places = jnp.arange(number_of)

    def named(tallies, rotation):
        used = int((tallies > 0).sum())
        fixed = max(1, used // 4)
        shifted = fixed + (places - fixed + rotation * (used - fixed)) % max(1, number_of - fixed)
        return jnp.zeros((number_of,), jnp.int32).at[ranking[jnp.where(places < fixed, places, shifted)]].set(jnp.asarray(tallies, jnp.int32))

    tallies = jnp.where(number % 4 == 0, named(heavy_load, number // 4), named(ordinary, number - number // 4 - 1))
    mixed = jax.random.permutation(jax.random.fold_in(own, 3), number_of)
    giver, taker = mixed[0:number_of // 2 * 2:2], mixed[1:number_of // 2 * 2:2]
    margin = jnp.minimum(tallies[giver] - 1, reach - tallies[taker]) // 2
    margin = jnp.where((giver == ranking[0]) | (taker == ranking[0]) | (tallies[taker] == 0), 0, jnp.maximum(margin, 0))
    shifted = jax.random.randint(jax.random.fold_in(own, 4), (number_of // 2,), 0, 1 << 20) % (margin + 1)
    tallies = tallies.at[giver].add(-shifted).at[taker].add(shifted)
    items = jnp.searchsorted(jnp.cumsum(tallies), jnp.arange(rows * top), side="right").astype(jnp.int32)
    table = items.reshape(top, rows).T
    table = table[jax.random.permutation(jax.random.fold_in(own, 1), rows)]
    rotation = jax.random.randint(jax.random.fold_in(own, 2), (rows, 1), 0, top)
    return jnp.take_along_axis(table, (jnp.arange(top)[None, :] + rotation) % top, axis=1)


def load_shares(amount, total, reach, skew, full):
    weights = [(1 << 20) // math.isqrt(grade ** skew) + 1 for grade in range(1, amount + 1)]
    largest = reach if full else min(reach, max(-(-total // amount), total * weights[0] // sum(weights)))
    least = 1 if total - largest >= amount - 1 else 0
    counts, surplus = [largest] + [least] * (amount - 1), total - largest - least * (amount - 1)
    while surplus > 0:
        candidates = [i for i in range(1, amount) if counts[i] < largest] or [i for i in range(1, amount) if counts[i] < reach]
        pool, left = sum([weights[i] for i in candidates]), surplus
        for i in candidates:
            extra = min(reach - counts[i], max(1, left * weights[i] // pool), surplus)
            counts[i] = counts[i] + extra
            surplus = surplus - extra
    return np.array(counts)


def normal_values(rng, shape, deviation, limit, pieces=(), kind=jnp.bfloat16):
    result = deviation * jax.random.normal(rng, shape, jnp.float32)
    if pieces:
        result = result * levels(rng, shape, pieces, -0.22, 0.18)
    return jnp.clip(result, -limit, limit).astype(kind)


def setup_inputs(seed: int = 0) -> dict:
    key_of = jax.random.split(jax.random.key(seed), 14)
    queries = draw_queries(jax.random.fold_in(key_of[13], 71), 0)
    prompt_cache = draw_prompt_cache(jax.random.fold_in(key_of[13], 71), 0)
    gen_cache = normal_values(key_of[2], (SAMPLES, GEN, KVH * 2 * HEAD), 1.0, 4.0, ((0, 64), (2, 8)))
    gen_lengths = uneven_parts(key_of[3], SAMPLES, SAMPLES * GEN // 2, GEN, 2).astype(jnp.int32)
    new_kv = normal_values(key_of[4], (SAMPLES, STEPS, KVH * 2 * HEAD), 1.0, 4.0, ((0, 64), (2, 8)))
    w_out = draw_w_out(jax.random.fold_in(key_of[13], 71), 0)
    residual = draw_residual(jax.random.fold_in(key_of[13], 71), 0)
    norm_gain = jnp.clip(1.0 + 0.1 * jax.random.normal(key_of[7], (D,), jnp.float32), 0.5, 1.5)
    w_gate = normal_values(key_of[8], (EXPERTS, D, FFE), D ** -0.5, 0.109375, ((0, 64), (2, 8)))
    w_up = normal_values(key_of[9], (EXPERTS, D, FFE), D ** -0.5, 0.109375, ((0, 64), (2, 8)))
    w_down = normal_values(key_of[10], (EXPERTS, FFE, D), FFE ** -0.5, 0.15625, ((0, 64), (1, 8)))
    expert_ids_keys = jax.random.split(jax.random.fold_in(key_of[11], 1), SAMPLES * STEPS // (SAMPLES * STEPS))
    expert_ids_turns = jax.random.permutation(jax.random.fold_in(key_of[11], 3), SAMPLES * STEPS // (SAMPLES * STEPS))
    expert_ids = jax.vmap(lambda own, number: routed_block(jax.random.fold_in(key_of[11], 2), own, number, SAMPLES * STEPS, EXPERTS, TOPK, MOSTE, 2))(expert_ids_keys, expert_ids_turns).reshape((SAMPLES, STEPS, TOPK))
    route_weights = jnp.clip(jax.random.uniform(key_of[12], (SAMPLES, STEPS, TOPK), jnp.float32, 0.05, 0.5), 0.05, 0.5)
    return dict(queries=queries, prompt_cache=prompt_cache, gen_cache=gen_cache, gen_lengths=gen_lengths, new_kv=new_kv, w_out=w_out, residual=residual, norm_gain=norm_gain, w_gate=w_gate, w_up=w_up, w_down=w_down, expert_ids=expert_ids, route_weights=route_weights)


def reference(queries, prompt_cache, gen_cache, gen_lengths, new_kv, w_out, residual, norm_gain, w_gate, w_up, w_down, expert_ids, route_weights):
    highest = lax.Precision.HIGHEST
    per_group = QH // KVH
    score_scale = HEAD ** (-0.5)
    query_all = queries.astype(jnp.float32).reshape(PROMPTS, GROUP, STEPS, KVH, per_group, HEAD)
    prompt_blocks = prompt_cache.reshape(PROMPTS, PLEN, KVH, 2, HEAD)
    gen_blocks = gen_cache.reshape(PROMPTS, GROUP, GEN, KVH, 2, HEAD)
    gen_lens = gen_lengths.reshape(PROMPTS, GROUP)
    fresh_blocks = new_kv.reshape(PROMPTS, GROUP, STEPS, KVH, 2, HEAD)

    def one_prompt(inputs):
        query_p, prompt_p, gen_p, lens_p, fresh_p = inputs
        prompt_p = prompt_p.astype(jnp.float32)
        gen_p = gen_p.astype(jnp.float32)
        fresh_p = fresh_p.astype(jnp.float32)
        prompt_scores = jnp.einsum('gtkrd,nkd->gtkrn', query_p, prompt_p[:, :, 0], precision=highest) * score_scale
        gen_scores = jnp.einsum('gtkrd,gnkd->gtkrn', query_p, gen_p[:, :, :, 0], precision=highest) * score_scale
        live_mask = jnp.arange(GEN)[None, :] < lens_p[:, None]
        gen_scores = jnp.where(live_mask[:, None, None, None, :], gen_scores, -jnp.inf)
        new_scores = jnp.einsum('gtkrd,gukd->gtkru', query_p, fresh_p[:, :, :, 0], precision=highest) * score_scale
        causal = jnp.arange(STEPS)[None, :] <= jnp.arange(STEPS)[:, None]
        new_scores = jnp.where(causal[None, :, None, None, :], new_scores, -jnp.inf)
        maxima = jnp.maximum(jnp.maximum(prompt_scores.max(-1), gen_scores.max(-1)), new_scores.max(-1))
        prompt_w = jnp.exp(prompt_scores - maxima[..., None])
        gen_w = jnp.exp(gen_scores - maxima[..., None])
        new_w = jnp.exp(new_scores - maxima[..., None])
        totals = prompt_w.sum(-1) + gen_w.sum(-1) + new_w.sum(-1)
        accumulated = jnp.einsum('gtkrn,nkd->gtkrd', prompt_w, prompt_p[:, :, 1], precision=highest)
        accumulated = accumulated + jnp.einsum('gtkrn,gnkd->gtkrd', gen_w, gen_p[:, :, :, 1], precision=highest)
        accumulated = accumulated + jnp.einsum('gtkru,gukd->gtkrd', new_w, fresh_p[:, :, :, 1], precision=highest)
        return (accumulated / totals[..., None]).astype(jnp.bfloat16)
    attended = lax.map(one_prompt, (query_all, prompt_blocks, gen_blocks, gen_lens, fresh_blocks))
    row_total = SAMPLES * STEPS
    heads_out = attended.reshape(row_total, QH * HEAD)
    projected = jnp.dot(heads_out, w_out, preferred_element_type=jnp.float32)
    residual_sum = residual.reshape(row_total, D).astype(jnp.float32) + projected
    inverse = lax.rsqrt(lax.optimization_barrier(jnp.mean(residual_sum * residual_sum, axis=1, keepdims=True)) + 1e-05)
    normed = (residual_sum * inverse * norm_gain).astype(jnp.bfloat16)
    route_ids = expert_ids.reshape(row_total, TOPK)
    route_w = route_weights.reshape(row_total, TOPK)

    def one_expert(running, expert):
        matches = route_ids == expert
        present = jnp.any(matches, axis=1)
        row_weight = lax.optimization_barrier(jnp.sum(jnp.where(matches, route_w, 0.0), axis=1))
        row_order = jnp.argsort(jnp.where(present, 0, 1).astype(jnp.int32), stable=True)[:MOSTE].astype(jnp.int32)
        chosen = normed[row_order]
        gate_pre = jnp.dot(chosen, w_gate[expert], preferred_element_type=jnp.float32)
        up_pre = jnp.dot(chosen, w_up[expert], preferred_element_type=jnp.float32)
        activation = (gate_pre * jax.nn.sigmoid(1.702 * gate_pre) * (up_pre + 1.0)).astype(jnp.bfloat16)
        expert_out = jnp.dot(activation, w_down[expert], preferred_element_type=jnp.float32)
        return (running.at[row_order].add(expert_out * row_weight[row_order][:, None]), None)
    expert_mix, _ = lax.scan(one_expert, jnp.zeros((row_total, D), jnp.float32), jnp.arange(EXPERTS, dtype=jnp.int32))
    return (residual_sum + expert_mix).astype(jnp.bfloat16).reshape(SAMPLES, STEPS, D)
```

```python
import jax
import jax.numpy as jnp
from jax import lax
from jax.experimental import pallas as pl
from jax.experimental.pallas import tpu as pltpu
from jax.sharding import PartitionSpec as P

D = 2880
HEAD = 64
MOSTE = 48
KV = 8
NX, NZ, NY, NC = 4, 2, 4, 2
SLICE = D // KV
LANES = 384
QUARTER = 720
WIDE = 768
PADDED = 2944
F32 = jnp.float32
BF16 = jnp.bfloat16
MESH = pl.DeviceIdType.MESH


def iota(shape, axis):
    return lax.broadcasted_iota(jnp.int32, shape, axis)


def onehot(mask):
    return jnp.where(mask, 1.0, 0.0).astype(BF16)


def dot(a, b, dims=((1,), (0,))):
    return lax.dot_general(a, b, (dims, ((), ())), preferred_element_type=F32)


def packed(m, l, acc):
    lane = iota(acc.shape, 1)
    return jnp.where(lane == 0, m, jnp.where(lane == 1, l, jnp.where(lane >= HEAD, acc, 0.0)))


def merge(rows):
    top = rows[0][:, 0:1]
    for r in rows[1:]:
        top = jnp.maximum(top, r[:, 0:1])
    total = rows[0] * jnp.exp(rows[0][:, 0:1] - top)
    for r in rows[1:]:
        total = total + r * jnp.exp(r[:, 0:1] - top)
    return jnp.where(iota(total.shape, 1) == 0, top, total)


def window(ref, k):
    start = SLICE * k // 128 * 128
    wide = ref[:, start:start + 512]
    shift = SLICE * k - start
    if shift:
        wide = pltpu.roll(wide, 512 - shift, 1)
    return wide[:, :LANES]


def kernel(
    q_ref, prompt_ref, gen_ref, new_ref, len_ref, wout_ref, res_ref, gain_ref,
    wg_ref, wu_ref, wd_ref, ids_ref, rw_ref, out_ref,
    qbuf, part, rc, s1, rx, s2, ry, s3, rz,
    proj, rsend, rrecv, agbuf, blk, ybuf, choose, shift_ref,
    oflat, esend, erecv, dn, r1, e1, rx2, e2, ry2, e3, rz2,
    send_sem, recv_sem,
):
    roll = lax.axis_index("roll")
    kv = lax.axis_index("kv")
    c = lax.rem(roll, NC)
    y = lax.rem(roll // NC, NY)
    z = lax.rem(roll // (NC * NY), NZ)
    x = roll // (NC * NY * NZ)

    def at(xx, zz, yy, cc):
        return (((xx * NZ + zz) * NY + yy) * NC + cc, kv)

    to_core = at(x, z, y, 1 - c)
    to_z = at(x, 1 - z, y, c)
    to_x = [at(lax.rem(x + d, NX), z, y, c) for d in range(1, NX)]
    to_y = [at(x, z, lax.rem(y + d, NY), c) for d in range(1, NY)]
    to_kv = [(roll, lax.rem(kv + d, KV)) for d in range(1, KV)]
    partners = [to_core, to_z] + to_x + to_y + to_kv
    barrier = pltpu.get_barrier_semaphore()
    for device in partners:
        pl.semaphore_signal(barrier, inc=1, device_id=device, device_id_type=MESH)

    next_sem = [0]

    def start(src, dst, device):
        i = next_sem[0]
        next_sem[0] += 1
        copy = pltpu.make_async_remote_copy(
            src_ref=src, dst_ref=dst, send_sem=send_sem.at[i], recv_sem=recv_sem.at[i],
            device_id=device, device_id_type=MESH,
        )
        copy.start()
        return copy

    def finish(copies):
        for copy in copies:
            copy.wait()

    def gather(buf):
        finish([start(buf.at[c, x, y, z], buf.at[c, x, y, z], to_z)])
        finish([start(buf.at[c, x, y], buf.at[c, x, y], device) for device in to_y])
        finish([start(buf.at[c, x], buf.at[c, x], device) for device in to_x])
        finish([start(buf.at[c], buf.at[c], to_core)])

    qbuf[c, x, y, z] = q_ref[...]

    match = ids_ref[...] == roll
    present = jnp.max(jnp.where(match, 1.0, 0.0), axis=0, keepdims=True)
    row_weight = jnp.sum(jnp.where(match, rw_ref[...], 0.0), axis=0, keepdims=True)
    present = jnp.broadcast_to(present, (16, 256))
    upto = onehot(iota((256, 256), 0) <= iota((256, 256), 1))
    slot = jnp.where(present > 0.5, dot(present.astype(BF16), upto) - 1.0, -1.0)
    row, col = iota((256, 1024), 0), iota((256, 1024), 1)
    spread = onehot(((row >> 2) == (col >> 4)) & ((row & 3) == (col & 3)))
    slot_wide = dot(slot.astype(BF16), spread)[0:1]
    lane = iota((1, 1024), 1)
    code = slot_wide + MOSTE * ((lane >> 2) & 3).astype(F32)
    code = jnp.where(slot_wide < -0.5, -1.0, code)
    choose[...] = onehot(iota((4 * MOSTE, 1024), 0) == code.astype(jnp.int32))
    chosen = iota((MOSTE, 256), 0) == slot[0:1].astype(jnp.int32)
    slot_weight = jnp.sum(jnp.where(chosen, row_weight, 0.0), axis=1, keepdims=True)
    back = onehot(chosen)
    row, col = iota((WIDE, WIDE), 0), iota((WIDE, WIDE), 1)
    shift_ref[...] = onehot(
        ((row < SLICE) & (col == row))
        | ((row >= LANES) & (row < LANES + SLICE) & (col == row - (LANES - SLICE)))
    )

    own = q_ref[...]
    live = iota((16, 128), 1) < len_ref[0]
    gen_s = jnp.where(live, dot(own, gen_ref[...], ((1,), (1,))), -1e30)
    causal = iota((16, 16), 1) <= (iota((16, 16), 0) & 3)
    new_s = jnp.where(causal, dot(own, new_ref[...], ((1,), (1,))), -1e30)
    top = jnp.maximum(
        jnp.max(gen_s, axis=1, keepdims=True), jnp.max(new_s, axis=1, keepdims=True)
    )
    gen_w = jnp.exp(gen_s - top)
    new_w = jnp.exp(new_s - top)
    own_part = packed(
        top,
        jnp.sum(gen_w, axis=1, keepdims=True) + jnp.sum(new_w, axis=1, keepdims=True),
        dot(gen_w.astype(BF16), gen_ref[...]) + dot(new_w.astype(BF16), new_ref[...]),
    )
    pl.semaphore_wait(barrier, len(partners))

    gather(qbuf)
    for cc in range(NC):
        for xx in range(NX):
            q = qbuf[cc, xx].reshape(128, 128)
            keys = prompt_ref[xx]
            s = dot(q, keys, ((1,), (1,)))
            m = jnp.max(s, axis=1, keepdims=True)
            w = jnp.exp(s - m)
            l = jnp.sum(w, axis=1, keepdims=True)
            part[cc, xx] = packed(m, l, dot(w.astype(BF16), keys)).reshape(NY, NZ, 16, 128)
    part[c, x, y, z] = merge([part[c, x, y, z], own_part])

    finish([start(part.at[1 - c], rc, to_core)])
    s1[...] = merge([part[c].reshape(512, 128), rc[...].reshape(512, 128)]).reshape(s1.shape)
    finish([
        start(s1.at[lax.rem(x + d, NX)], rx.at[d - 1], to_x[d - 1]) for d in range(1, NX)
    ])
    s2[...] = merge(
        [s1[x].reshape(128, 128)] + [rx[d].reshape(128, 128) for d in range(NX - 1)]
    ).reshape(s2.shape)
    finish([
        start(s2.at[lax.rem(y + d, NY)], ry.at[d - 1], to_y[d - 1]) for d in range(1, NY)
    ])
    s3[...] = merge(
        [s2[y].reshape(32, 128)] + [ry[d].reshape(32, 128) for d in range(NY - 1)]
    ).reshape(s3.shape)
    finish([start(s3.at[1 - z], rz, to_z)])
    final = merge([s3[z], rz[...]])
    lane = iota((16, 128), 1)
    attended = jnp.where(lane >= HEAD, final / final[:, 1:2], 0.0).astype(BF16)

    row, col = iota((128, 256), 0), iota((128, 256), 1)
    copies = onehot((row >= HEAD) & ((col & (HEAD - 1)) == row - HEAD))
    heads = dot(attended, copies)
    heads = jnp.where((iota((16, 256), 0) >> 2) == (iota((16, 256), 1) >> 6), heads, 0.0)
    steps = onehot((iota((16, 16), 1) & 3) == iota((16, 16), 0))
    attended = dot(steps, heads.astype(BF16)).astype(BF16)
    proj[:, PADDED - 128:] = jnp.zeros((8, 128), F32)
    proj[:, :D] = dot(attended, wout_ref[...])[0:8]
    for k in range(KV):
        rsend[k] = window(proj, k).astype(BF16)
    finish([
        start(rsend.at[lax.rem(kv + d, KV)], rrecv.at[d - 1], to_kv[d - 1])
        for d in range(1, KV)
    ])
    projected = rsend[kv].astype(F32)
    for d in range(KV - 1):
        projected = projected + rrecv[d].astype(F32)
    lane = iota((8, LANES), 1)
    residual_sum = jnp.where(lane < SLICE, res_ref[...] + projected, 0.0)

    squares = jnp.sum(residual_sum * residual_sum, axis=1, keepdims=True)
    high = squares.astype(BF16).astype(F32)
    scaled = residual_sum * gain_ref[...]
    agbuf[kv] = jnp.where(
        lane == SLICE, high, jnp.where(lane == SLICE + 1, squares - high, scaled)
    ).astype(BF16)
    finish([start(agbuf.at[kv], agbuf.at[kv], device) for device in to_kv])
    squares = jnp.zeros((8, 1), F32)
    for k in range(KV):
        piece = agbuf[k].astype(F32)
        squares = squares + piece[:, SLICE:SLICE + 1] + piece[:, SLICE + 1:SLICE + 2]
        half = LANES * (k % 2)
        blk[4 * (k // 2):4 * (k // 2) + 4, half:half + LANES] = piece[0:4]
    inverse = lax.rsqrt(squares / D + 1e-05)
    inverse = jnp.concatenate([inverse, inverse], axis=0)
    high = inverse.astype(BF16).astype(F32)
    block = dot(blk[...].astype(BF16), shift_ref[...])
    lane = iota((16, WIDE), 1)
    ybuf[c, x, y, z] = jnp.where(
        lane == QUARTER, high, jnp.where(lane == QUARTER + 1, inverse - high, block)
    ).astype(BF16)
    gather(ybuf)

    rows = dot(choose[...], ybuf[...].reshape(1024, WIDE))
    factor = rows[0:MOSTE, QUARTER:QUARTER + 1] + rows[0:MOSTE, QUARTER + 1:QUARTER + 2]
    gate = jnp.zeros((MOSTE, wg_ref.shape[1]), F32)
    up = jnp.zeros((MOSTE, wg_ref.shape[1]), F32)
    for j in range(4):
        features = rows[MOSTE * j:MOSTE * (j + 1), :QUARTER].astype(BF16)
        gate = gate + dot(features, wg_ref[QUARTER * j:QUARTER * (j + 1), :])
        up = up + dot(features, wu_ref[QUARTER * j:QUARTER * (j + 1), :])
    gate = gate * factor
    up = up * factor
    activation = (gate * jax.nn.sigmoid(1.702 * gate) * (up + 1.0)).astype(BF16)
    oflat[:, PADDED - 128:] = jnp.zeros((MOSTE, 128), F32)
    oflat[:, :D] = dot(activation, wd_ref[...]) * slot_weight
    for k in range(KV):
        esend[k] = window(oflat, k).astype(BF16)
    finish([
        start(esend.at[lax.rem(kv + d, KV)], erecv.at[d - 1], to_kv[d - 1])
        for d in range(1, KV)
    ])
    summed = esend[kv].astype(F32)
    for d in range(KV - 1):
        summed = summed + erecv[d].astype(F32)

    dense = dot(back, summed.astype(BF16), ((0,), (0,)))
    dn[...] = dense.astype(BF16).reshape(dn.shape)
    finish([start(dn.at[1 - c], r1, to_core)])
    e1[...] = (dn[c].astype(F32) + r1[...].astype(F32)).reshape(e1.shape)
    finish([
        start(e1.at[lax.rem(x + d, NX)], rx2.at[d - 1], to_x[d - 1]) for d in range(1, NX)
    ])
    e2[...] = (e1[x] + rx2[0] + rx2[1] + rx2[2]).reshape(e2.shape)
    finish([
        start(e2.at[lax.rem(y + d, NY)], ry2.at[d - 1], to_y[d - 1]) for d in range(1, NY)
    ])
    e3[...] = e2[y] + ry2[0] + ry2[1] + ry2[2]
    finish([start(e3, rz2, to_z)])
    mix = e3[...] + rz2[...]
    mix = jnp.where(z == 0, mix, pltpu.roll(mix, 4, 0))
    out_ref[...] = residual_sum + mix


def on_device(
    queries, prompt_cache, gen_cache, gen_lengths, new_kv, w_out, residual, norm_gain,
    w_gate, w_up, w_down, expert_ids, route_weights,
):
    steps = queries.shape[1]
    q = queries.reshape(steps, 4, HEAD).transpose(1, 0, 2).reshape(4 * steps, HEAD)
    q = jnp.pad(q * BF16(0.125), ((0, 0), (0, HEAD)))
    fresh = jnp.pad(new_kv[0], ((0, 16 - steps), (0, 0)))
    res = jnp.pad(residual[0].astype(F32), ((0, 8 - steps), (0, LANES - SLICE)))
    gain = jnp.pad(norm_gain, (0, LANES - SLICE)).reshape(1, LANES)

    def by_device(a):
        a = a.reshape(NX, NZ, NY, NC, steps, 4)
        return a.transpose(5, 3, 0, 2, 1, 4).reshape(4, -1)

    vmem = pl.BlockSpec(memory_space=pltpu.VMEM)
    smem = pl.BlockSpec(memory_space=pltpu.SMEM)
    grid = (NC, NX, NY, NZ)
    ffe = w_gate.shape[2]
    scratch = [
        pltpu.VMEM(grid + (16, 128), BF16),
        pltpu.VMEM(grid + (16, 128), F32),
        pltpu.VMEM((NX, NY, NZ, 16, 128), F32),
        pltpu.VMEM((NX, NY, NZ, 16, 128), F32),
        pltpu.VMEM((NX - 1, NY, NZ, 16, 128), F32),
        pltpu.VMEM((NY, NZ, 16, 128), F32),
        pltpu.VMEM((NY - 1, NZ, 16, 128), F32),
        pltpu.VMEM((NZ, 16, 128), F32),
        pltpu.VMEM((16, 128), F32),
        pltpu.VMEM((8, PADDED), F32),
        pltpu.VMEM((KV, 8, LANES), BF16),
        pltpu.VMEM((KV - 1, 8, LANES), BF16),
        pltpu.VMEM((KV, 8, LANES), BF16),
        pltpu.VMEM((16, WIDE), F32),
        pltpu.VMEM(grid + (16, WIDE), BF16),
        pltpu.VMEM((4 * MOSTE, 1024), BF16),
        pltpu.VMEM((WIDE, WIDE), BF16),
        pltpu.VMEM((MOSTE, PADDED), F32),
        pltpu.VMEM((KV, MOSTE, LANES), BF16),
        pltpu.VMEM((KV - 1, MOSTE, LANES), BF16),
        pltpu.VMEM((NC, 128, LANES), BF16),
        pltpu.VMEM((128, LANES), BF16),
        pltpu.VMEM((NX, 32, LANES), F32),
        pltpu.VMEM((NX - 1, 32, LANES), F32),
        pltpu.VMEM((NY, 8, LANES), F32),
        pltpu.VMEM((NY - 1, 8, LANES), F32),
        pltpu.VMEM((8, LANES), F32),
        pltpu.VMEM((8, LANES), F32),
        pltpu.SemaphoreType.DMA((64,)),
        pltpu.SemaphoreType.DMA((64,)),
    ]
    out = pl.pallas_call(
        kernel,
        out_shape=jax.ShapeDtypeStruct((8, LANES), F32),
        in_specs=[vmem] * 4 + [smem] + [vmem] * 8,
        out_specs=vmem,
        scratch_shapes=scratch,
        compiler_params=pltpu.CompilerParams(
            collective_id=0, has_side_effects=True, vmem_limit_bytes=56 * 1024 * 1024
        ),
        name="layer",
    )(
        q, prompt_cache, gen_cache[0], fresh, gen_lengths, w_out, res, gain,
        w_gate.reshape(D, ffe), w_up.reshape(D, ffe), w_down.reshape(ffe, D),
        by_device(expert_ids), by_device(route_weights),
    )
    return out[:steps, :SLICE].astype(BF16)[None]


def solution(mesh):
    in_specs = (
        P("roll", None, "kv"),
        P(None, "roll", "kv"),
        P("roll", None, "kv"),
        P("roll"),
        P("roll", None, "kv"),
        P("kv", None),
        P("roll", None, "kv"),
        P("kv"),
        P("roll", None, "kv"),
        P("roll", None, "kv"),
        P("roll", "kv", None),
        P(),
        P(),
    )
    out_specs = P("roll", None, "kv")
    return jax.shard_map(
        on_device, mesh=mesh, in_specs=in_specs, out_specs=out_specs, check_vma=False
    )
```

```python
import jax
import jax.numpy as jnp
from jax import lax
from jax.experimental import pallas as pl
from jax.experimental.pallas import tpu as pltpu
from jax.sharding import PartitionSpec as P

D = 2880
HEAD = 64
MOSTE = 48
KV = 8
NX, NZ, NY, NC = 4, 2, 4, 2
SLICE = D // KV
LANES = 384
QUARTER = 720
WIDE = 768
PADDED = 2944
F32 = jnp.float32
BF16 = jnp.bfloat16
MESH = pl.DeviceIdType.MESH


def iota(shape, axis):
    return lax.broadcasted_iota(jnp.int32, shape, axis)


def onehot(mask):
    return jnp.where(mask, 1.0, 0.0).astype(BF16)


def dot(a, b, dims=((1,), (0,))):
    return lax.dot_general(a, b, (dims, ((), ())), preferred_element_type=F32)


def packed(m, l, acc):
    lane = iota(acc.shape, 1)
    return jnp.where(lane == 0, m, jnp.where(lane == 1, l, jnp.where(lane >= HEAD, acc, 0.0)))


def merge(rows):
    top = rows[0][:, 0:1]
    for r in rows[1:]:
        top = jnp.maximum(top, r[:, 0:1])
    total = rows[0] * jnp.exp(rows[0][:, 0:1] - top)
    for r in rows[1:]:
        total = total + r * jnp.exp(r[:, 0:1] - top)
    return jnp.where(iota(total.shape, 1) == 0, top, total)


def window(ref, k):
    start = SLICE * k // 128 * 128
    wide = ref[:, start:start + 512]
    shift = SLICE * k - start
    if shift:
        wide = pltpu.roll(wide, 512 - shift, 1)
    return wide[:, :LANES]


def kernel(
    q_ref, prompt_hbm, gen_hbm, new_ref, len_ref, wout_hbm, res_ref, gain_ref,
    wg_hbm, wu_hbm, wd_hbm, ids_ref, rw_ref, out_ref,
    prompt_ref, gen_ref, wout_ref, wg_ref, wu_ref, wd_ref,
    padq, padn, padr, padg, pres,
    qbuf, part, rc, s1, rx, s2, ry, s3, rz,
    proj, rsend, rrecv, agbuf, blk, ybuf, choose, shift_ref, xs,
    oflat, esend, erecv, dn, r1, e1, rx2, e2, ry2, e3, rz2,
    send_sem, recv_sem, load_sem,
):
    roll = lax.axis_index("roll")
    kv = lax.axis_index("kv")
    c = lax.rem(roll, NC)
    y = lax.rem(roll // NC, NY)
    z = lax.rem(roll // (NC * NY), NZ)
    x = roll // (NC * NY * NZ)

    def at(xx, zz, yy, cc):
        return (((xx * NZ + zz) * NY + yy) * NC + cc, kv)

    to_core = at(x, z, y, 1 - c)
    to_z = at(x, 1 - z, y, c)
    to_x = [at(lax.rem(x + d, NX), z, y, c) for d in range(1, NX)]
    to_y = [at(x, z, lax.rem(y + d, NY), c) for d in range(1, NY)]
    to_kv = [(roll, lax.rem(kv + d, KV)) for d in range(1, KV)]
    column = z * KV + kv
    to_column = []
    for d in range(1, NZ * KV):
        there = lax.rem(column + d, NZ * KV)
        to_column.append((at(x, there // KV, y, c)[0], lax.rem(there, KV)))
    partners = [to_core] + to_x + to_y + to_column
    barrier = pltpu.get_barrier_semaphore()
    for device in partners:
        pl.semaphore_signal(barrier, inc=1, device_id=device, device_id_type=MESH)

    loads = [
        pltpu.make_async_copy(src, dst, load_sem.at[i])
        for i, (src, dst) in enumerate([
            (gen_hbm, gen_ref), (prompt_hbm, prompt_ref), (wout_hbm, wout_ref),
            (wg_hbm, wg_ref), (wu_hbm, wu_ref), (wd_hbm, wd_ref),
        ])
    ]
    for load in loads:
        load.start()

    next_sem = [0]

    def start(src, dst, device):
        i = next_sem[0]
        next_sem[0] += 1
        copy = pltpu.make_async_remote_copy(
            src_ref=src, dst_ref=dst, send_sem=send_sem.at[i], recv_sem=recv_sem.at[i],
            device_id=device, device_id_type=MESH,
        )
        copy.start()
        return copy

    def finish(copies):
        for copy in copies:
            copy.wait()

    padq[...] = jnp.zeros((16, 256), F32)
    padq[0:4, :] = q_ref[...].astype(F32) * 0.125
    row, col = iota((128, 256), 0), iota((128, 256), 1)
    own_head = (iota((16, 256), 0) >> 2) == (iota((16, 256), 1) >> 6)
    each = dot(onehot((iota((16, 16), 0) & 3) == iota((16, 16), 1)), padq[...].astype(BF16))
    each = jnp.where(own_head, each, 0.0).astype(BF16)
    fold = onehot((row < HEAD) & ((col & (HEAD - 1)) == row))
    own = dot(each, fold, ((1,), (1,))).astype(BF16)
    qbuf[z, c, x, y] = own

    pres[...] = jnp.zeros((16, 64), F32)
    weights = []
    for t in range(4):
        match = ids_ref[t] == roll
        pres[t:t + 1, :] = jnp.max(jnp.where(match, 1.0, 0.0), axis=0, keepdims=True)
        weights.append(jnp.sum(jnp.where(match, rw_ref[t], 0.0), axis=0, keepdims=True))
    present = pres[...]
    upto = onehot(iota((64, 64), 0) <= iota((64, 64), 1))
    earlier = onehot(iota((16, 16), 1) < iota((16, 16), 0))
    totals = jnp.broadcast_to(jnp.sum(present, axis=1, keepdims=True), (16, 64))
    slot = dot(present.astype(BF16), upto) + dot(earlier, totals.astype(BF16)) - 1.0
    slot = jnp.where(present > 0.5, slot, -1.0)
    slot_half = slot.astype(BF16)

    def place(sample):
        return (
            (((sample >> 3) & 1) << 5) | ((sample & 1) << 4)
            | ((sample >> 4) << 2) | ((sample >> 1) & 3)
        )

    spread = onehot(place(iota((64, 1024), 0)) == (iota((64, 1024), 1) >> 4))
    wide = dot(slot_half, spread)
    wide = jnp.where(iota((16, 1024), 0) == (iota((16, 1024), 1) & 3), wide, 0.0)
    wide = jnp.sum(wide, axis=0, keepdims=True)
    lane = iota((1, 1024), 1)
    code = jnp.where(wide < -0.5, -1.0, wide + MOSTE * ((lane >> 2) & 3).astype(F32))
    choose[...] = onehot(iota((4 * MOSTE, 1024), 0) == code.astype(jnp.int32))
    spread = onehot(place(iota((64, 256), 0)) == (iota((64, 256), 1) >> 2))
    wide = dot(slot_half, spread)
    wide = jnp.where(iota((16, 256), 0) == (iota((16, 256), 1) & 3), wide, 0.0)
    wide = jnp.sum(wide, axis=0, keepdims=True).astype(jnp.int32)
    back = onehot(iota((MOSTE, 256), 0) == wide)
    slot_weight = jnp.zeros((MOSTE, 1), F32)
    slot_whole = slot.astype(jnp.int32)
    for t in range(4):
        mine = iota((MOSTE, 64), 0) == slot_whole[t:t + 1]
        slot_weight = slot_weight + jnp.sum(
            jnp.where(mine, weights[t], 0.0), axis=1, keepdims=True
        )
    row, col = iota((WIDE, WIDE), 0), iota((WIDE, WIDE), 1)
    shift_ref[...] = onehot(
        ((row < SLICE) & (col == row))
        | ((row >= LANES) & (row < LANES + SLICE + 2) & (col == row - (LANES - SLICE)))
    )

    padn[...] = jnp.zeros((16, 128), F32)
    padn[0:4, :] = new_ref[...].astype(F32)
    fresh = padn[...].astype(BF16)
    loads[0].wait()
    live = iota((16, 128), 1) < len_ref[0]
    gen_s = jnp.where(live, dot(own, gen_ref[...], ((1,), (1,))), -1e30)
    causal = iota((16, 16), 1) <= (iota((16, 16), 0) & 3)
    new_s = jnp.where(causal, dot(own, fresh, ((1,), (1,))), -1e30)
    top = jnp.maximum(
        jnp.max(gen_s, axis=1, keepdims=True), jnp.max(new_s, axis=1, keepdims=True)
    )
    gen_w = jnp.exp(gen_s - top)
    new_w = jnp.exp(new_s - top)
    own_part = packed(
        top,
        jnp.sum(gen_w, axis=1, keepdims=True) + jnp.sum(new_w, axis=1, keepdims=True),
        dot(gen_w.astype(BF16), gen_ref[...]) + dot(new_w.astype(BF16), fresh),
    )
    padr[...] = jnp.zeros((8, LANES), F32)
    padr[0:4, 0:SLICE] = res_ref[...].astype(F32)
    padg[...] = jnp.zeros((1, LANES), F32)
    padg[:, 0:SLICE] = gain_ref[...]
    pl.semaphore_wait(barrier, len(partners))

    def attend(h):
        for cc in range(NC):
            for xx in range(NX):
                keys = prompt_ref[xx]
                s = dot(qbuf[h, cc, xx].reshape(64, 128), keys, ((1,), (1,)))
                m = jnp.max(s, axis=1, keepdims=True)
                w = jnp.exp(s - m)
                l = jnp.sum(w, axis=1, keepdims=True)
                part[h, cc, xx] = packed(m, l, dot(w.astype(BF16), keys)).reshape(NY, 16, 128)

    def share_y(h):
        return [start(qbuf.at[h, c, x, y], qbuf.at[h, c, x, y], device) for device in to_y]

    def share_x(h):
        return [start(qbuf.at[h, c, x], qbuf.at[h, c, x], device) for device in to_x]

    def share_core(h):
        return [start(qbuf.at[h, c], qbuf.at[h, c], to_core)]

    def sum_core(i, h):
        return [start(part.at[h, 1 - c], rc.at[i], to_core)]

    def add_core(i, h):
        rows = (NX * NY * 16, 128)
        s1[i] = merge([part[h, c].reshape(rows), rc[i].reshape(rows)]).reshape(s1.shape[1:])

    def sum_x(i):
        return [
            start(s1.at[i, lax.rem(x + d, NX)], rx.at[i, d - 1], to_x[d - 1])
            for d in range(1, NX)
        ]

    def add_x(i):
        rows = (NY * 16, 128)
        s2[i] = merge(
            [s1[i, x].reshape(rows)] + [rx[i, d].reshape(rows) for d in range(NX - 1)]
        ).reshape(s2.shape[1:])

    def sum_y(i):
        return [
            start(s2.at[i, lax.rem(y + d, NY)], ry.at[i, d - 1], to_y[d - 1])
            for d in range(1, NY)
        ]

    def add_y(i):
        s3[i] = merge([s2[i, y]] + [ry[i, d] for d in range(NY - 1)])

    far = 1 - z
    across = [start(qbuf.at[z, c, x, y], qbuf.at[z, c, x, y], to_z)]
    finish(share_y(z))
    finish(share_x(z))
    finish(share_core(z))
    loads[1].wait()
    attend(z)
    part[z, c, x, y] = merge([part[z, c, x, y], own_part])
    near = sum_core(0, z)
    finish(across)
    flight = share_y(far)
    finish(near)
    add_core(0, z)
    near = sum_x(0)
    finish(flight)
    flight = share_x(far)
    finish(near)
    add_x(0)
    near = sum_y(0)
    finish(flight)
    flight = share_core(far)
    finish(near)
    add_y(0)
    finish(flight)
    attend(far)
    finish(sum_core(1, far))
    add_core(1, far)
    finish(sum_x(1))
    add_x(1)
    finish(sum_y(1))
    add_y(1)
    finish([start(s3.at[1], rz, to_z)])
    final = merge([s3[0], rz[...]])
    lane = iota((16, 128), 1)
    attended = jnp.where(lane >= HEAD, final / final[:, 1:2], 0.0).astype(BF16)

    row, col = iota((128, 256), 0), iota((128, 256), 1)
    copies = onehot((row >= HEAD) & ((col & (HEAD - 1)) == row - HEAD))
    heads = jnp.where(own_head, dot(attended, copies), 0.0)
    steps = onehot((iota((16, 16), 1) & 3) == iota((16, 16), 0))
    attended = dot(steps, heads.astype(BF16)).astype(BF16)
    proj[:, PADDED - 128:] = jnp.zeros((8, 128), F32)
    loads[2].wait()
    proj[:, :D] = dot(attended, wout_ref[...], ((1,), (1,)))[0:8]
    for k in range(KV):
        rsend[k] = window(proj, k)[0:4].astype(BF16)
    finish([
        start(rsend.at[lax.rem(kv + d, KV)], rrecv.at[d - 1], to_kv[d - 1])
        for d in range(1, KV)
    ])
    projected = rsend[kv].astype(F32)
    for d in range(KV - 1):
        projected = projected + rrecv[d].astype(F32)
    lane = iota((4, LANES), 1)
    residual_sum = jnp.where(lane < SLICE, padr[0:4, :] + projected, 0.0)

    squares = jnp.sum(residual_sum * residual_sum, axis=1, keepdims=True)
    high = squares.astype(BF16).astype(F32)
    scaled = residual_sum * padg[...]
    agbuf[column] = jnp.where(
        lane == SLICE, high, jnp.where(lane == SLICE + 1, squares - high, scaled)
    ).astype(BF16)
    finish([start(agbuf.at[column], agbuf.at[column], device) for device in to_column])
    for zz in range(NZ):
        pieces = [agbuf[KV * zz + k].astype(F32) for k in range(KV)]
        squares = jnp.zeros((4, 1), F32)
        for piece in pieces:
            squares = squares + piece[:, SLICE:SLICE + 1] + piece[:, SLICE + 1:SLICE + 2]
        inverse = lax.rsqrt(squares / D + 1e-05)
        high = inverse.astype(BF16).astype(F32)
        for k, piece in enumerate(pieces):
            piece = jnp.where(
                lane == SLICE, high, jnp.where(lane == SLICE + 1, inverse - high, piece)
            )
            low, half = 16 * zz + 4 * (k // 2), LANES * (k % 2)
            blk[low:low + 4, half:half + LANES] = piece
    block = dot(blk[...].astype(BF16), shift_ref[...]).astype(BF16)
    ybuf[0, c, x, y] = block[0:16]
    ybuf[1, c, x, y] = block[16:32]

    a = [start(ybuf.at[0, c, x, y], ybuf.at[0, c, x, y], device) for device in to_y]
    b = [start(ybuf.at[1, c, x, y], ybuf.at[1, c, x, y], device) for device in to_x]
    finish(a)
    a = [start(ybuf.at[0, c, x], ybuf.at[0, c, x], device) for device in to_x]
    finish(b)
    b = [start(ybuf.at[1, c, :, y], ybuf.at[1, c, :, y], device) for device in to_y]
    finish(a)
    a = [start(ybuf.at[0, c], ybuf.at[0, c], to_core)]
    finish(b)
    b = [start(ybuf.at[1, c], ybuf.at[1, c], to_core)]
    for load in loads[3:]:
        load.wait()
    finish(a)
    finish(b)

    rows = dot(choose[...], ybuf[...].reshape(1024, WIDE))
    factor = rows[0:MOSTE, QUARTER:QUARTER + 1] + rows[0:MOSTE, QUARTER + 1:QUARTER + 2]
    xs[...] = jnp.zeros(xs.shape, F32)
    for j in range(4):
        low = QUARTER * j // 128 * 128
        features = jnp.where(
            iota((MOSTE, WIDE), 1) < QUARTER, rows[MOSTE * j:MOSTE * (j + 1)], 0.0
        )
        features = jnp.concatenate([features, jnp.zeros((MOSTE, 128), F32)], axis=1)
        if QUARTER * j - low:
            features = pltpu.roll(features, QUARTER * j - low, 1)
        xs[:, low:low + WIDE + 128] += features
    features = xs[:, :D].astype(BF16)
    gate = dot(features, wg_ref[...], ((1,), (1,))) * factor
    up = dot(features, wu_ref[...], ((1,), (1,))) * factor
    activation = (gate * jax.nn.sigmoid(1.702 * gate) * (up + 1.0)).astype(BF16)
    oflat[:, PADDED - 128:] = jnp.zeros((MOSTE, 128), F32)
    oflat[:, :D] = dot(activation, wd_ref[...]) * slot_weight
    for k in range(KV):
        esend[k] = window(oflat, k).astype(BF16)
    finish([
        start(esend.at[lax.rem(kv + d, KV)], erecv.at[d - 1], to_kv[d - 1])
        for d in range(1, KV)
    ])
    summed = esend[kv].astype(F32)
    for d in range(KV - 1):
        summed = summed + erecv[d].astype(F32)

    dense = dot(back, summed.astype(BF16), ((0,), (0,)))
    dn[...] = dense.astype(BF16).reshape(dn.shape)

    def fold_half(i, h):
        finish([start(dn.at[h, 1 - c], r1.at[i], to_core)])
        e1[i] = (dn[h, c].astype(F32) + r1[i].astype(F32)).reshape(NX, 16, LANES)
        finish([
            start(e1.at[i, lax.rem(x + d, NX)], rx2.at[i, d - 1], to_x[d - 1])
            for d in range(1, NX)
        ])
        total = e1[i, x] + rx2[i, 0] + rx2[i, 1] + rx2[i, 2]
        for yy in range(NY):
            e2[i, yy] = total[4 * yy:4 * yy + 4]
        finish([
            start(e2.at[i, lax.rem(y + d, NY)], ry2.at[i, d - 1], to_y[d - 1])
            for d in range(1, NY)
        ])
        e3[i] = e2[i, y] + ry2[i, 0] + ry2[i, 1] + ry2[i, 2]

    fold_half(1, far)
    across = [start(e3.at[1], rz2, to_z)]
    fold_half(0, z)
    finish(across)
    out = residual_sum + e3[0] + rz2[...]
    out_ref[...] = out[:, 0:SLICE].astype(BF16)


def on_device(
    queries, prompt_cache, gen_cache, gen_lengths, new_kv, w_out, residual, norm_gain,
    w_gate, w_up, w_down, expert_ids, route_weights,
):
    ffe = w_gate.shape[2]
    anywhere = pl.BlockSpec(memory_space=pl.ANY)
    vmem = pl.BlockSpec(memory_space=pltpu.VMEM)
    smem = pl.BlockSpec(memory_space=pltpu.SMEM)
    grid = (NZ, NC, NX, NY)
    scratch = [
        pltpu.VMEM(prompt_cache.shape, BF16),
        pltpu.VMEM(gen_cache.shape[1:], BF16),
        pltpu.VMEM((D, 256), BF16),
        pltpu.VMEM((ffe, D), BF16),
        pltpu.VMEM((ffe, D), BF16),
        pltpu.VMEM((ffe, D), BF16),
        pltpu.VMEM((16, 256), F32),
        pltpu.VMEM((16, 128), F32),
        pltpu.VMEM((8, LANES), F32),
        pltpu.VMEM((1, LANES), F32),
        pltpu.VMEM((16, 64), F32),
        pltpu.VMEM(grid + (16, 128), BF16),
        pltpu.VMEM(grid + (16, 128), F32),
        pltpu.VMEM((2, NX, NY, 16, 128), F32),
        pltpu.VMEM((2, NX, NY, 16, 128), F32),
        pltpu.VMEM((2, NX - 1, NY, 16, 128), F32),
        pltpu.VMEM((2, NY, 16, 128), F32),
        pltpu.VMEM((2, NY - 1, 16, 128), F32),
        pltpu.VMEM((2, 16, 128), F32),
        pltpu.VMEM((16, 128), F32),
        pltpu.VMEM((8, PADDED), F32),
        pltpu.VMEM((KV, 4, LANES), BF16),
        pltpu.VMEM((KV - 1, 4, LANES), BF16),
        pltpu.VMEM((NZ * KV, 4, LANES), BF16),
        pltpu.VMEM((32, WIDE), F32),
        pltpu.VMEM(grid + (16, WIDE), BF16),
        pltpu.VMEM((4 * MOSTE, 1024), BF16),
        pltpu.VMEM((WIDE, WIDE), BF16),
        pltpu.VMEM((MOSTE, PADDED), F32),
        pltpu.VMEM((MOSTE, PADDED), F32),
        pltpu.VMEM((KV, MOSTE, LANES), BF16),
        pltpu.VMEM((KV - 1, MOSTE, LANES), BF16),
        pltpu.VMEM((NZ, NC, 64, LANES), BF16),
        pltpu.VMEM((2, 64, LANES), BF16),
        pltpu.VMEM((2, NX, 16, LANES), F32),
        pltpu.VMEM((2, NX - 1, 16, LANES), F32),
        pltpu.VMEM((2, NY, 4, LANES), F32),
        pltpu.VMEM((2, NY - 1, 4, LANES), F32),
        pltpu.VMEM((2, 4, LANES), F32),
        pltpu.VMEM((4, LANES), F32),
        pltpu.SemaphoreType.DMA((96,)),
        pltpu.SemaphoreType.DMA((96,)),
        pltpu.SemaphoreType.DMA((6,)),
    ]
    out = pl.pallas_call(
        kernel,
        out_shape=jax.ShapeDtypeStruct(residual.shape[1:], BF16),
        in_specs=[vmem, anywhere, anywhere, vmem, smem, anywhere, vmem, vmem]
        + [anywhere] * 3 + [vmem] * 2,
        out_specs=vmem,
        scratch_shapes=scratch,
        compiler_params=pltpu.CompilerParams(
            collective_id=0, has_side_effects=True, vmem_limit_bytes=60 * 1024 * 1024
        ),
        name="layer",
    )(
        queries[0], prompt_cache, gen_cache[0], new_kv[0], gen_lengths, w_out.T, residual[0],
        norm_gain.reshape(1, SLICE), w_gate[0].T, w_up[0].T, w_down[0],
        expert_ids.transpose(1, 2, 0), route_weights.transpose(1, 2, 0),
    )
    return out[None]


def solution(mesh):
    in_specs = (
        P("roll", None, "kv"),
        P(None, "roll", "kv"),
        P("roll", None, "kv"),
        P("roll"),
        P("roll", None, "kv"),
        P("kv", None),
        P("roll", None, "kv"),
        P("kv"),
        P("roll", None, "kv"),
        P("roll", None, "kv"),
        P("roll", "kv", None),
        P(),
        P(),
    )
    out_specs = P("roll", None, "kv")
    return jax.shard_map(
        on_device, mesh=mesh, in_specs=in_specs, out_specs=out_specs, check_vma=False
    )
```

```python
import jax
import jax.numpy as jnp
from jax import lax
from jax.experimental import pallas as pl
from jax.experimental.pallas import tpu as pltpu
from jax.sharding import PartitionSpec as P

D = 2880
HEAD = 64
MOSTE = 48
KV = 8
NX, NZ, NY, NC = 4, 2, 4, 2
SLICE = D // KV
LANES = 384
QUARTER = 720
WIDE = 768
PADDED = 2944
F32 = jnp.float32
BF16 = jnp.bfloat16
MESH = pl.DeviceIdType.MESH


def iota(shape, axis):
    return lax.broadcasted_iota(jnp.int32, shape, axis)


def onehot(mask):
    return jnp.where(mask, 1.0, 0.0).astype(BF16)


def dot(a, b, dims=((1,), (0,))):
    return lax.dot_general(a, b, (dims, ((), ())), preferred_element_type=F32)


def packed(m, l, acc):
    lane = iota(acc.shape, 1)
    return jnp.where(lane == 0, m, jnp.where(lane == 1, l, jnp.where(lane >= HEAD, acc, 0.0)))


def merge(rows):
    top = rows[0][:, 0:1]
    for r in rows[1:]:
        top = jnp.maximum(top, r[:, 0:1])
    total = rows[0] * jnp.exp(rows[0][:, 0:1] - top)
    for r in rows[1:]:
        total = total + r * jnp.exp(r[:, 0:1] - top)
    return jnp.where(iota(total.shape, 1) == 0, top, total)


def window(ref, k):
    start = SLICE * k // 128 * 128
    wide = ref[:, start:start + 512]
    shift = SLICE * k - start
    if shift:
        wide = pltpu.roll(wide, 512 - shift, 1)
    return wide[:, :LANES]


def kernel(
    q_ref, prompt_hbm, gen_hbm, new_ref, len_ref, wout_hbm, res_ref, gain_ref,
    wg_hbm, wu_hbm, wd_hbm, ids_ref, rw_ref, out_ref,
    prompt_ref, gen_ref, wout_ref, wg_ref, wu_ref, wd_ref,
    padq, padn, padr, padg, pres,
    qbuf, part, rc, s1, rx, s2, ry, s3, rz,
    proj, rsend, rrecv, agbuf, blk, ybuf, choose, xs,
    oflat, esend, erecv, dn, r1, e1, rx2, e2, ry2, e3, rz2,
    send_sem, recv_sem, load_sem,
):
    roll = lax.axis_index("roll")
    kv = lax.axis_index("kv")
    c = lax.rem(roll, NC)
    y = lax.rem(roll // NC, NY)
    z = lax.rem(roll // (NC * NY), NZ)
    x = roll // (NC * NY * NZ)

    def at(xx, zz, yy, cc):
        return (((xx * NZ + zz) * NY + yy) * NC + cc, kv)

    to_core = at(x, z, y, 1 - c)
    to_z = at(x, 1 - z, y, c)
    to_x = [at(lax.rem(x + d, NX), z, y, c) for d in range(1, NX)]
    to_y = [at(x, z, lax.rem(y + d, NY), c) for d in range(1, NY)]
    to_kv = [(roll, lax.rem(kv + d, KV)) for d in range(1, KV)]
    column = z * KV + kv
    to_column = []
    for d in range(1, NZ * KV):
        there = lax.rem(column + d, NZ * KV)
        to_column.append((at(x, there // KV, y, c)[0], lax.rem(there, KV)))
    partners = [to_core] + to_x + to_y + to_column
    barrier = pltpu.get_barrier_semaphore()
    for device in partners:
        pl.semaphore_signal(barrier, inc=1, device_id=device, device_id_type=MESH)

    loads = [
        pltpu.make_async_copy(src, dst, load_sem.at[i])
        for i, (src, dst) in enumerate([
            (gen_hbm, gen_ref), (prompt_hbm, prompt_ref), (wout_hbm, wout_ref),
            (wg_hbm, wg_ref), (wu_hbm, wu_ref), (wd_hbm, wd_ref),
        ])
    ]
    for load in loads:
        load.start()

    next_sem = [0]

    def start(src, dst, device):
        i = next_sem[0]
        next_sem[0] += 1
        copy = pltpu.make_async_remote_copy(
            src_ref=src, dst_ref=dst, send_sem=send_sem.at[i], recv_sem=recv_sem.at[i],
            device_id=device, device_id_type=MESH,
        )
        copy.start()
        return copy

    def finish(copies):
        for copy in copies:
            copy.wait()

    padq[...] = jnp.zeros((16, 256), F32)
    padq[0:4, :] = q_ref[...].astype(F32) * 0.125
    row, col = iota((128, 256), 0), iota((128, 256), 1)
    own_head = (iota((16, 256), 0) >> 2) == (iota((16, 256), 1) >> 6)
    each = dot(onehot((iota((16, 16), 0) & 3) == iota((16, 16), 1)), padq[...].astype(BF16))
    each = jnp.where(own_head, each, 0.0).astype(BF16)
    fold = onehot((row < HEAD) & ((col & (HEAD - 1)) == row))
    own = dot(each, fold, ((1,), (1,))).astype(BF16)
    qbuf[z, c, x, y] = own

    pres[...] = jnp.zeros((16, 64), F32)
    weights = []
    for t in range(4):
        match = ids_ref[t] == roll
        pres[t:t + 1, :] = jnp.max(jnp.where(match, 1.0, 0.0), axis=0, keepdims=True)
        weights.append(jnp.sum(jnp.where(match, rw_ref[t], 0.0), axis=0, keepdims=True))
    present = pres[...]
    upto = onehot(iota((64, 64), 0) <= iota((64, 64), 1))
    earlier = onehot(iota((16, 16), 1) < iota((16, 16), 0))
    totals = jnp.broadcast_to(jnp.sum(present, axis=1, keepdims=True), (16, 64))
    slot = dot(present.astype(BF16), upto) + dot(earlier, totals.astype(BF16)) - 1.0
    slot = jnp.where(present > 0.5, slot, -1.0)
    slot_half = slot.astype(BF16)

    def place(sample):
        return (
            (((sample >> 3) & 1) << 5) | ((sample & 1) << 4)
            | ((sample >> 4) << 2) | ((sample >> 1) & 3)
        )

    padr[...] = jnp.zeros((8, LANES), F32)
    padr[0:4, 0:SLICE] = res_ref[...].astype(F32)
    padg[...] = jnp.zeros((1, LANES), F32)
    padg[:, 0:SLICE] = gain_ref[...]
    pl.semaphore_wait(barrier, len(partners))

    def attend(h):
        scores = []
        for xx in range(NX):
            q = jnp.concatenate([qbuf[h, cc, xx].reshape(64, 128) for cc in range(NC)], axis=0)
            scores.append(dot(q, prompt_ref[xx], ((1,), (1,))))
        tops = [jnp.max(s, axis=1, keepdims=True) for s in scores]
        scores = [jnp.exp(s - m) for s, m in zip(scores, tops)]
        totals = [jnp.sum(w, axis=1, keepdims=True) for w in scores]
        for xx in range(NX):
            values = dot(scores[xx].astype(BF16), prompt_ref[xx])
            rows = packed(tops[xx], totals[xx], values)
            for cc in range(NC):
                part[h, cc, xx] = rows[64 * cc:64 * (cc + 1)].reshape(NY, 16, 128)

    def share_y(h):
        return [start(qbuf.at[h, c, x, y], qbuf.at[h, c, x, y], device) for device in to_y]

    def share_x(h):
        return [start(qbuf.at[h, c, x], qbuf.at[h, c, x], device) for device in to_x]

    def share_core(h):
        return [start(qbuf.at[h, c], qbuf.at[h, c], to_core)]

    def sum_core(i, h):
        return [start(part.at[h, 1 - c], rc.at[i], to_core)]

    def add_core(i, h):
        rows = (NX * NY * 16, 128)
        s1[i] = merge([part[h, c].reshape(rows), rc[i].reshape(rows)]).reshape(s1.shape[1:])

    def sum_x(i):
        return [
            start(s1.at[i, lax.rem(x + d, NX)], rx.at[i, d - 1], to_x[d - 1])
            for d in range(1, NX)
        ]

    def add_x(i):
        rows = (NY * 16, 128)
        s2[i] = merge(
            [s1[i, x].reshape(rows)] + [rx[i, d].reshape(rows) for d in range(NX - 1)]
        ).reshape(s2.shape[1:])

    def sum_y(i):
        return [
            start(s2.at[i, lax.rem(y + d, NY)], ry.at[i, d - 1], to_y[d - 1])
            for d in range(1, NY)
        ]

    def add_y(i):
        s3[i] = merge([s2[i, y]] + [ry[i, d] for d in range(NY - 1)])

    far = 1 - z
    across = [start(qbuf.at[z, c, x, y], qbuf.at[z, c, x, y], to_z)]
    flight = share_y(z)
    padn[...] = jnp.zeros((16, 128), F32)
    padn[0:4, :] = new_ref[...].astype(F32)
    fresh = padn[...].astype(BF16)
    loads[0].wait()
    live = iota((16, 128), 1) < len_ref[0]
    gen_s = jnp.where(live, dot(own, gen_ref[...], ((1,), (1,))), -1e30)
    causal = iota((16, 16), 1) <= (iota((16, 16), 0) & 3)
    new_s = jnp.where(causal, dot(own, fresh, ((1,), (1,))), -1e30)
    top = jnp.maximum(
        jnp.max(gen_s, axis=1, keepdims=True), jnp.max(new_s, axis=1, keepdims=True)
    )
    gen_w = jnp.exp(gen_s - top)
    new_w = jnp.exp(new_s - top)
    own_part = packed(
        top,
        jnp.sum(gen_w, axis=1, keepdims=True) + jnp.sum(new_w, axis=1, keepdims=True),
        dot(gen_w.astype(BF16), gen_ref[...]) + dot(new_w.astype(BF16), fresh),
    )
    finish(flight)
    finish(share_x(z))
    finish(share_core(z))
    finish(across)
    flight = share_y(far)
    loads[1].wait()
    attend(z)
    part[z, c, x, y] = merge([part[z, c, x, y], own_part])
    near = sum_core(0, z)
    finish(flight)
    flight = share_x(far)
    finish(near)
    add_core(0, z)
    near = sum_x(0)
    finish(flight)
    flight = share_core(far)
    finish(near)
    add_x(0)
    near = sum_y(0)
    finish(flight)
    attend(far)
    flight = sum_core(1, far)
    finish(near)
    add_y(0)
    finish(flight)
    add_core(1, far)
    finish(sum_x(1))
    add_x(1)
    finish(sum_y(1))
    add_y(1)
    flight = [start(s3.at[1], rz, to_z)]
    spread = onehot(place(iota((64, 1024), 0)) == (iota((64, 1024), 1) >> 4))
    wide = dot(slot_half, spread)
    wide = jnp.where(iota((16, 1024), 0) == (iota((16, 1024), 1) & 3), wide, 0.0)
    wide = jnp.sum(wide, axis=0, keepdims=True)
    lane = iota((1, 1024), 1)
    code = jnp.where(wide < -0.5, -1.0, wide + MOSTE * ((lane >> 2) & 3).astype(F32))
    choose[...] = onehot(iota((4 * MOSTE, 1024), 0) == code.astype(jnp.int32))
    spread = onehot(place(iota((64, 256), 0)) == (iota((64, 256), 1) >> 2))
    wide = dot(slot_half, spread)
    wide = jnp.where(iota((16, 256), 0) == (iota((16, 256), 1) & 3), wide, 0.0)
    wide = jnp.sum(wide, axis=0, keepdims=True).astype(jnp.int32)
    back = onehot(iota((MOSTE, 256), 0) == wide)
    slot_weight = jnp.zeros((MOSTE, 1), F32)
    slot_whole = slot.astype(jnp.int32)
    for t in range(4):
        mine = iota((MOSTE, 64), 0) == slot_whole[t:t + 1]
        slot_weight = slot_weight + jnp.sum(
            jnp.where(mine, weights[t], 0.0), axis=1, keepdims=True
        )
    finish(flight)
    final = merge([s3[0], rz[...]])
    lane = iota((16, 128), 1)
    attended = jnp.where(lane >= HEAD, final / final[:, 1:2], 0.0).astype(BF16)

    row, col = iota((128, 256), 0), iota((128, 256), 1)
    copies = onehot((row >= HEAD) & ((col & (HEAD - 1)) == row - HEAD))
    heads = jnp.where(own_head, dot(attended, copies), 0.0)
    steps = onehot((iota((16, 16), 1) & 3) == iota((16, 16), 0))
    attended = dot(steps, heads.astype(BF16)).astype(BF16)
    proj[:, PADDED - 128:] = jnp.zeros((8, 128), F32)
    loads[2].wait()
    proj[:, :D] = dot(attended, wout_ref[...], ((1,), (1,)))[0:8]
    for k in range(KV):
        rsend[k] = window(proj, k)[0:4].astype(BF16)
    finish([
        start(rsend.at[lax.rem(kv + d, KV)], rrecv.at[d - 1], to_kv[d - 1])
        for d in range(1, KV)
    ])
    projected = rsend[kv].astype(F32)
    for d in range(KV - 1):
        projected = projected + rrecv[d].astype(F32)
    lane = iota((4, LANES), 1)
    residual_sum = jnp.where(lane < SLICE, padr[0:4, :] + projected, 0.0)

    squares = jnp.sum(residual_sum * residual_sum, axis=1, keepdims=True)
    high = squares.astype(BF16).astype(F32)
    scaled = residual_sum * padg[...]
    agbuf[column] = jnp.where(
        lane == SLICE, high, jnp.where(lane == SLICE + 1, squares - high, scaled)
    ).astype(BF16)
    finish([start(agbuf.at[column], agbuf.at[column], device) for device in to_column])
    for zz in range(NZ):
        pieces = [agbuf[KV * zz + k].astype(F32) for k in range(KV)]
        squares = jnp.zeros((4, 1), F32)
        for piece in pieces:
            squares = squares + piece[:, SLICE:SLICE + 1] + piece[:, SLICE + 1:SLICE + 2]
        inverse = lax.rsqrt(squares / D + 1e-05)
        high = inverse.astype(BF16).astype(F32)
        for k, piece in enumerate(pieces):
            piece = jnp.where(
                lane == SLICE, high, jnp.where(lane == SLICE + 1, inverse - high, piece)
            )
            low, half = 16 * zz + 4 * (k // 2), LANES * (k % 2)
            blk[low:low + 4, half:half + LANES] = piece
    block = blk[...]
    block = jnp.where(
        iota(block.shape, 1) < SLICE, block, pltpu.roll(block, WIDE - (LANES - SLICE), 1)
    ).astype(BF16)
    ybuf[0, c, x, y] = block[0:16]
    ybuf[1, c, x, y] = block[16:32]

    a = [start(ybuf.at[0, c, x, y], ybuf.at[0, c, x, y], device) for device in to_y]
    b = [start(ybuf.at[1, c, x, y], ybuf.at[1, c, x, y], device) for device in to_x]
    finish(a)
    a = [start(ybuf.at[0, c, x], ybuf.at[0, c, x], device) for device in to_x]
    finish(b)
    b = [start(ybuf.at[1, c, :, y], ybuf.at[1, c, :, y], device) for device in to_y]
    finish(a)
    a = [start(ybuf.at[0, c], ybuf.at[0, c], to_core)]
    finish(b)
    b = [start(ybuf.at[1, c], ybuf.at[1, c], to_core)]
    for load in loads[3:]:
        load.wait()
    finish(a)
    finish(b)

    rows = dot(choose[...], ybuf[...].reshape(1024, WIDE))
    factor = rows[0:MOSTE, QUARTER:QUARTER + 1] + rows[0:MOSTE, QUARTER + 1:QUARTER + 2]
    xs[...] = jnp.zeros(xs.shape, F32)
    for j in range(4):
        low = QUARTER * j // 128 * 128
        features = jnp.where(
            iota((MOSTE, WIDE), 1) < QUARTER, rows[MOSTE * j:MOSTE * (j + 1)], 0.0
        )
        features = jnp.concatenate([features, jnp.zeros((MOSTE, 128), F32)], axis=1)
        if QUARTER * j - low:
            features = pltpu.roll(features, QUARTER * j - low, 1)
        xs[:, low:low + WIDE + 128] += features
    features = xs[:, :D].astype(BF16)
    gate = dot(features, wg_ref[...], ((1,), (1,))) * factor
    up = dot(features, wu_ref[...], ((1,), (1,))) * factor
    activation = (gate * jax.nn.sigmoid(1.702 * gate) * (up + 1.0)).astype(BF16)
    oflat[:, PADDED - 128:] = jnp.zeros((MOSTE, 128), F32)
    oflat[:, :D] = dot(activation, wd_ref[...]) * slot_weight
    for k in range(KV):
        esend[k] = window(oflat, k).astype(BF16)
    finish([
        start(esend.at[lax.rem(kv + d, KV)], erecv.at[d - 1], to_kv[d - 1])
        for d in range(1, KV)
    ])
    summed = esend[kv].astype(F32)
    for d in range(KV - 1):
        summed = summed + erecv[d].astype(F32)

    dense = dot(back, summed.astype(BF16), ((0,), (0,)))
    dn[...] = dense.astype(BF16).reshape(dn.shape)

    def fold_half(i, h):
        finish([start(dn.at[h, 1 - c], r1.at[i], to_core)])
        e1[i] = (dn[h, c].astype(F32) + r1[i].astype(F32)).reshape(NX, 16, LANES)
        finish([
            start(e1.at[i, lax.rem(x + d, NX)], rx2.at[i, d - 1], to_x[d - 1])
            for d in range(1, NX)
        ])
        total = e1[i, x] + rx2[i, 0] + rx2[i, 1] + rx2[i, 2]
        for yy in range(NY):
            e2[i, yy] = total[4 * yy:4 * yy + 4]
        finish([
            start(e2.at[i, lax.rem(y + d, NY)], ry2.at[i, d - 1], to_y[d - 1])
            for d in range(1, NY)
        ])
        e3[i] = e2[i, y] + ry2[i, 0] + ry2[i, 1] + ry2[i, 2]

    fold_half(1, far)
    across = [start(e3.at[1], rz2, to_z)]
    fold_half(0, z)
    finish(across)
    out = residual_sum + e3[0] + rz2[...]
    out_ref[...] = out[:, 0:SLICE].astype(BF16)


def on_device(
    queries, prompt_cache, gen_cache, gen_lengths, new_kv, w_out, residual, norm_gain,
    w_gate, w_up, w_down, expert_ids, route_weights,
):
    ffe = w_gate.shape[2]
    anywhere = pl.BlockSpec(memory_space=pl.ANY)
    vmem = pl.BlockSpec(memory_space=pltpu.VMEM)
    smem = pl.BlockSpec(memory_space=pltpu.SMEM)
    grid = (NZ, NC, NX, NY)
    scratch = [
        pltpu.VMEM(prompt_cache.shape, BF16),
        pltpu.VMEM(gen_cache.shape[1:], BF16),
        pltpu.VMEM((D, 256), BF16),
        pltpu.VMEM((ffe, D), BF16),
        pltpu.VMEM((ffe, D), BF16),
        pltpu.VMEM((ffe, D), BF16),
        pltpu.VMEM((16, 256), F32),
        pltpu.VMEM((16, 128), F32),
        pltpu.VMEM((8, LANES), F32),
        pltpu.VMEM((1, LANES), F32),
        pltpu.VMEM((16, 64), F32),
        pltpu.VMEM(grid + (16, 128), BF16),
        pltpu.VMEM(grid + (16, 128), F32),
        pltpu.VMEM((2, NX, NY, 16, 128), F32),
        pltpu.VMEM((2, NX, NY, 16, 128), F32),
        pltpu.VMEM((2, NX - 1, NY, 16, 128), F32),
        pltpu.VMEM((2, NY, 16, 128), F32),
        pltpu.VMEM((2, NY - 1, 16, 128), F32),
        pltpu.VMEM((2, 16, 128), F32),
        pltpu.VMEM((16, 128), F32),
        pltpu.VMEM((8, PADDED), F32),
        pltpu.VMEM((KV, 4, LANES), BF16),
        pltpu.VMEM((KV - 1, 4, LANES), BF16),
        pltpu.VMEM((NZ * KV, 4, LANES), BF16),
        pltpu.VMEM((32, WIDE), F32),
        pltpu.VMEM(grid + (16, WIDE), BF16),
        pltpu.VMEM((4 * MOSTE, 1024), BF16),
        pltpu.VMEM((MOSTE, PADDED), F32),
        pltpu.VMEM((MOSTE, PADDED), F32),
        pltpu.VMEM((KV, MOSTE, LANES), BF16),
        pltpu.VMEM((KV - 1, MOSTE, LANES), BF16),
        pltpu.VMEM((NZ, NC, 64, LANES), BF16),
        pltpu.VMEM((2, 64, LANES), BF16),
        pltpu.VMEM((2, NX, 16, LANES), F32),
        pltpu.VMEM((2, NX - 1, 16, LANES), F32),
        pltpu.VMEM((2, NY, 4, LANES), F32),
        pltpu.VMEM((2, NY - 1, 4, LANES), F32),
        pltpu.VMEM((2, 4, LANES), F32),
        pltpu.VMEM((4, LANES), F32),
        pltpu.SemaphoreType.DMA((96,)),
        pltpu.SemaphoreType.DMA((96,)),
        pltpu.SemaphoreType.DMA((6,)),
    ]
    out = pl.pallas_call(
        kernel,
        out_shape=jax.ShapeDtypeStruct(residual.shape[1:], BF16),
        in_specs=[vmem, anywhere, anywhere, vmem, smem, anywhere, vmem, vmem]
        + [anywhere] * 3 + [vmem] * 2,
        out_specs=vmem,
        scratch_shapes=scratch,
        compiler_params=pltpu.CompilerParams(
            collective_id=0, has_side_effects=True, vmem_limit_bytes=60 * 1024 * 1024
        ),
        name="layer",
    )(
        queries[0], prompt_cache, gen_cache[0], new_kv[0], gen_lengths, w_out.T, residual[0],
        norm_gain.reshape(1, SLICE), w_gate[0].T, w_up[0].T, w_down[0],
        expert_ids.transpose(1, 2, 0), route_weights.transpose(1, 2, 0),
    )
    return out[None]


def solution(mesh):
    in_specs = (
        P("roll", None, "kv"),
        P(None, "roll", "kv"),
        P("roll", None, "kv"),
        P("roll"),
        P("roll", None, "kv"),
        P("kv", None),
        P("roll", None, "kv"),
        P("kv"),
        P("roll", None, "kv"),
        P("roll", None, "kv"),
        P("roll", "kv", None),
        P(),
        P(),
    )
    out_specs = P("roll", None, "kv")
    return jax.shard_map(
        on_device, mesh=mesh, in_specs=in_specs, out_specs=out_specs, check_vma=False
    )
```

```python
import jax
import jax.numpy as jnp
from jax import lax
from jax.experimental import pallas as pl
from jax.experimental.pallas import tpu as pltpu
from jax.sharding import PartitionSpec as P

D = 2880
HEAD = 64
MOSTE = 48
KV = 8
NX, NZ, NY, NC = 4, 2, 4, 2
SLICE = D // KV
LANES = 384
QUARTER = 720
WIDE = 768
PADDED = 2944
F32 = jnp.float32
BF16 = jnp.bfloat16
MESH = pl.DeviceIdType.MESH


def iota(shape, axis):
    return lax.broadcasted_iota(jnp.int32, shape, axis)


def onehot(mask):
    return jnp.where(mask, 1.0, 0.0).astype(BF16)


def dot(a, b, dims=((1,), (0,))):
    return lax.dot_general(a, b, (dims, ((), ())), preferred_element_type=F32)


def packed(m, l, acc):
    lane = iota(acc.shape, 1)
    return jnp.where(lane == 0, m, jnp.where(lane == 1, l, jnp.where(lane >= HEAD, acc, 0.0)))


def merge(rows):
    top = rows[0][:, 0:1]
    for r in rows[1:]:
        top = jnp.maximum(top, r[:, 0:1])
    total = rows[0] * jnp.exp(rows[0][:, 0:1] - top)
    for r in rows[1:]:
        total = total + r * jnp.exp(r[:, 0:1] - top)
    return jnp.where(iota(total.shape, 1) == 0, top, total)


def window(ref, k):
    start = SLICE * k // 128 * 128
    wide = ref[:, start:start + 512]
    shift = SLICE * k - start
    if shift:
        wide = pltpu.roll(wide, 512 - shift, 1)
    return wide[:, :LANES]


def kernel(
    q_ref, prompt_hbm, gen_hbm, new_ref, len_ref, wout_hbm, res_ref, gain_ref,
    wg_hbm, wu_hbm, wd_hbm, ids_ref, rw_ref, out_ref,
    prompt_ref, gen_ref, wout_ref, wg_ref, wu_ref, wd_ref,
    padq, padn, padr, padg, pres,
    qbuf, part, rc, s1, rx, s3, rz,
    proj, rsend, rrecv, agbuf, blk, ybuf, choose, xs,
    oflat, esend, erecv, dn, r1, e1, rx2, e3, rz2,
    send_sem, recv_sem, load_sem,
):
    roll = lax.axis_index("roll")
    kv = lax.axis_index("kv")
    c = lax.rem(roll, NC)
    y = lax.rem(roll // NC, NY)
    z = lax.rem(roll // (NC * NY), NZ)
    x = roll // (NC * NY * NZ)

    def at(xx, zz, yy, cc):
        return (((xx * NZ + zz) * NY + yy) * NC + cc, kv)

    to_core = at(x, z, y, 1 - c)
    to_z = at(x, 1 - z, y, c)
    to_x = [at(lax.rem(x + d, NX), z, y, c) for d in range(1, NX)]
    to_y = [at(x, z, lax.rem(y + d, NY), c) for d in range(1, NY)]
    others = [(dx, dy) for dx in range(NX) for dy in range(NY) if dx or dy]
    in_plane = [(lax.rem(x + dx, NX), lax.rem(y + dy, NY)) for dx, dy in others]
    to_plane = [at(xx, z, yy, c) for xx, yy in in_plane]
    to_kv = [(roll, lax.rem(kv + d, KV)) for d in range(1, KV)]
    column = z * KV + kv
    to_column = []
    for d in range(1, NZ * KV):
        there = lax.rem(column + d, NZ * KV)
        to_column.append((at(x, there // KV, y, c)[0], lax.rem(there, KV)))
    partners = [to_core] + to_plane + to_column
    barrier = pltpu.get_barrier_semaphore()
    for device in partners:
        pl.semaphore_signal(barrier, inc=1, device_id=device, device_id_type=MESH)

    loads = [
        pltpu.make_async_copy(src, dst, load_sem.at[i])
        for i, (src, dst) in enumerate([
            (gen_hbm, gen_ref), (prompt_hbm, prompt_ref), (wout_hbm, wout_ref),
            (wg_hbm, wg_ref), (wu_hbm, wu_ref), (wd_hbm, wd_ref),
        ])
    ]
    for load in loads:
        load.start()

    next_sem = [0]

    def start(src, dst, device):
        i = next_sem[0]
        next_sem[0] += 1
        copy = pltpu.make_async_remote_copy(
            src_ref=src, dst_ref=dst, send_sem=send_sem.at[i], recv_sem=recv_sem.at[i],
            device_id=device, device_id_type=MESH,
        )
        copy.start()
        return copy

    def finish(copies):
        for copy in copies:
            copy.wait()

    padq[...] = jnp.zeros((16, 256), F32)
    padq[0:4, :] = q_ref[...].astype(F32) * 0.125
    row, col = iota((128, 256), 0), iota((128, 256), 1)
    own_head = (iota((16, 256), 0) >> 2) == (iota((16, 256), 1) >> 6)
    each = dot(onehot((iota((16, 16), 0) & 3) == iota((16, 16), 1)), padq[...].astype(BF16))
    each = jnp.where(own_head, each, 0.0).astype(BF16)
    fold = onehot((row < HEAD) & ((col & (HEAD - 1)) == row))
    own = dot(each, fold, ((1,), (1,))).astype(BF16)
    qbuf[z, c, x, y] = own

    pres[...] = jnp.zeros((16, 64), F32)
    weights = []
    for t in range(4):
        match = ids_ref[t] == roll
        pres[t:t + 1, :] = jnp.max(jnp.where(match, 1.0, 0.0), axis=0, keepdims=True)
        weights.append(jnp.sum(jnp.where(match, rw_ref[t], 0.0), axis=0, keepdims=True))
    present = pres[...]
    upto = onehot(iota((64, 64), 0) <= iota((64, 64), 1))
    earlier = onehot(iota((16, 16), 1) < iota((16, 16), 0))
    totals = jnp.broadcast_to(jnp.sum(present, axis=1, keepdims=True), (16, 64))
    slot = dot(present.astype(BF16), upto) + dot(earlier, totals.astype(BF16)) - 1.0
    slot = jnp.where(present > 0.5, slot, -1.0)
    slot_half = slot.astype(BF16)

    def place(sample):
        return (
            (((sample >> 3) & 1) << 5) | ((sample & 1) << 4)
            | ((sample >> 4) << 2) | ((sample >> 1) & 3)
        )

    padr[...] = jnp.zeros((8, LANES), F32)
    padr[0:4, 0:SLICE] = res_ref[...].astype(F32)
    padg[...] = jnp.zeros((1, LANES), F32)
    padg[:, 0:SLICE] = gain_ref[...]
    pl.semaphore_wait(barrier, len(partners))

    def attend(h):
        scores = []
        for xx in range(NX):
            q = jnp.concatenate([qbuf[h, cc, xx].reshape(64, 128) for cc in range(NC)], axis=0)
            scores.append(dot(q, prompt_ref[xx], ((1,), (1,))))
        tops = [jnp.max(s, axis=1, keepdims=True) for s in scores]
        scores = [jnp.exp(s - m) for s, m in zip(scores, tops)]
        totals = [jnp.sum(w, axis=1, keepdims=True) for w in scores]
        for xx in range(NX):
            values = dot(scores[xx].astype(BF16), prompt_ref[xx])
            rows = packed(tops[xx], totals[xx], values)
            for cc in range(NC):
                part[h, cc, xx] = rows[64 * cc:64 * (cc + 1)].reshape(NY, 16, 128)

    def share_plane(h):
        return [start(qbuf.at[h, c, x, y], qbuf.at[h, c, x, y], device) for device in to_plane]

    def share_core(h):
        return [start(qbuf.at[h, c], qbuf.at[h, c], to_core)]

    def sum_core(i, h):
        return [start(part.at[h, 1 - c], rc.at[i], to_core)]

    def add_core(i, h):
        rows = (NX * NY * 16, 128)
        s1[i] = merge([part[h, c].reshape(rows), rc[i].reshape(rows)]).reshape(s1.shape[1:])

    def sum_plane(i):
        return [
            start(s1.at[i, xx, yy], rx.at[i, k], to_plane[k])
            for k, (xx, yy) in enumerate(in_plane)
        ]

    def add_plane(i):
        s3[i] = merge([s1[i, x, y]] + [rx[i, k] for k in range(len(others))])

    far = 1 - z
    across = [start(qbuf.at[z, c, x, y], qbuf.at[z, c, x, y], to_z)]
    flight = share_plane(z)
    padn[...] = jnp.zeros((16, 128), F32)
    padn[0:4, :] = new_ref[...].astype(F32)
    fresh = padn[...].astype(BF16)
    loads[0].wait()
    live = iota((16, 128), 1) < len_ref[0]
    gen_s = jnp.where(live, dot(own, gen_ref[...], ((1,), (1,))), -1e30)
    causal = iota((16, 16), 1) <= (iota((16, 16), 0) & 3)
    new_s = jnp.where(causal, dot(own, fresh, ((1,), (1,))), -1e30)
    top = jnp.maximum(
        jnp.max(gen_s, axis=1, keepdims=True), jnp.max(new_s, axis=1, keepdims=True)
    )
    gen_w = jnp.exp(gen_s - top)
    new_w = jnp.exp(new_s - top)
    own_part = packed(
        top,
        jnp.sum(gen_w, axis=1, keepdims=True) + jnp.sum(new_w, axis=1, keepdims=True),
        dot(gen_w.astype(BF16), gen_ref[...]) + dot(new_w.astype(BF16), fresh),
    )
    finish(flight)
    finish(share_core(z))
    finish(across)
    flight = share_plane(far)
    loads[1].wait()
    attend(z)
    part[z, c, x, y] = merge([part[z, c, x, y], own_part])
    near = sum_core(0, z)
    finish(flight)
    flight = share_core(far)
    finish(near)
    add_core(0, z)
    near = sum_plane(0)
    finish(flight)
    attend(far)
    flight = sum_core(1, far)
    finish(near)
    add_plane(0)
    finish(flight)
    add_core(1, far)
    finish(sum_plane(1))
    add_plane(1)
    flight = [start(s3.at[1], rz, to_z)]
    spread = onehot(place(iota((64, 1024), 0)) == (iota((64, 1024), 1) >> 4))
    wide = dot(slot_half, spread)
    wide = jnp.where(iota((16, 1024), 0) == (iota((16, 1024), 1) & 3), wide, 0.0)
    wide = jnp.sum(wide, axis=0, keepdims=True)
    lane = iota((1, 1024), 1)
    code = jnp.where(wide < -0.5, -1.0, wide + MOSTE * ((lane >> 2) & 3).astype(F32))
    choose[...] = onehot(iota((4 * MOSTE, 1024), 0) == code.astype(jnp.int32))
    spread = onehot(place(iota((64, 256), 0)) == (iota((64, 256), 1) >> 2))
    wide = dot(slot_half, spread)
    wide = jnp.where(iota((16, 256), 0) == (iota((16, 256), 1) & 3), wide, 0.0)
    wide = jnp.sum(wide, axis=0, keepdims=True).astype(jnp.int32)
    back = onehot(iota((MOSTE, 256), 0) == wide)
    slot_weight = jnp.zeros((MOSTE, 1), F32)
    slot_whole = slot.astype(jnp.int32)
    for t in range(4):
        mine = iota((MOSTE, 64), 0) == slot_whole[t:t + 1]
        slot_weight = slot_weight + jnp.sum(
            jnp.where(mine, weights[t], 0.0), axis=1, keepdims=True
        )
    finish(flight)
    final = merge([s3[0], rz[...]])
    lane = iota((16, 128), 1)
    attended = jnp.where(lane >= HEAD, final / final[:, 1:2], 0.0).astype(BF16)

    row, col = iota((128, 256), 0), iota((128, 256), 1)
    copies = onehot((row >= HEAD) & ((col & (HEAD - 1)) == row - HEAD))
    heads = jnp.where(own_head, dot(attended, copies), 0.0)
    steps = onehot((iota((16, 16), 1) & 3) == iota((16, 16), 0))
    attended = dot(steps, heads.astype(BF16)).astype(BF16)
    proj[:, PADDED - 128:] = jnp.zeros((8, 128), F32)
    loads[2].wait()
    proj[:, :D] = dot(attended, wout_ref[...], ((1,), (1,)))[0:8]
    for k in range(KV):
        rsend[k] = window(proj, k)[0:4].astype(BF16)
    finish([
        start(rsend.at[lax.rem(kv + d, KV)], rrecv.at[d - 1], to_kv[d - 1])
        for d in range(1, KV)
    ])
    projected = rsend[kv].astype(F32)
    for d in range(KV - 1):
        projected = projected + rrecv[d].astype(F32)
    lane = iota((4, LANES), 1)
    residual_sum = jnp.where(lane < SLICE, padr[0:4, :] + projected, 0.0)

    squares = jnp.sum(residual_sum * residual_sum, axis=1, keepdims=True)
    high = squares.astype(BF16).astype(F32)
    scaled = residual_sum * padg[...]
    agbuf[column] = jnp.where(
        lane == SLICE, high, jnp.where(lane == SLICE + 1, squares - high, scaled)
    ).astype(BF16)
    finish([start(agbuf.at[column], agbuf.at[column], device) for device in to_column])
    for zz in range(NZ):
        pieces = [agbuf[KV * zz + k].astype(F32) for k in range(KV)]
        squares = jnp.zeros((4, 1), F32)
        for piece in pieces:
            squares = squares + piece[:, SLICE:SLICE + 1] + piece[:, SLICE + 1:SLICE + 2]
        inverse = lax.rsqrt(squares / D + 1e-05)
        high = inverse.astype(BF16).astype(F32)
        for k, piece in enumerate(pieces):
            piece = jnp.where(
                lane == SLICE, high, jnp.where(lane == SLICE + 1, inverse - high, piece)
            )
            low, half = 16 * zz + 4 * (k // 2), LANES * (k % 2)
            blk[low:low + 4, half:half + LANES] = piece
    block = blk[...]
    block = jnp.where(
        iota(block.shape, 1) < SLICE, block, pltpu.roll(block, WIDE - (LANES - SLICE), 1)
    ).astype(BF16)
    ybuf[0, c, x, y] = block[0:16]
    ybuf[1, c, x, y] = block[16:32]

    a = [start(ybuf.at[0, c, x, y], ybuf.at[0, c, x, y], device) for device in to_y]
    b = [start(ybuf.at[1, c, x, y], ybuf.at[1, c, x, y], device) for device in to_x]
    finish(a)
    a = [start(ybuf.at[0, c, x], ybuf.at[0, c, x], device) for device in to_x]
    finish(b)
    b = [start(ybuf.at[1, c, :, y], ybuf.at[1, c, :, y], device) for device in to_y]
    finish(a)
    a = [start(ybuf.at[0, c], ybuf.at[0, c], to_core)]
    finish(b)
    b = [start(ybuf.at[1, c], ybuf.at[1, c], to_core)]
    for load in loads[3:]:
        load.wait()
    finish(a)
    finish(b)

    rows = dot(choose[...], ybuf[...].reshape(1024, WIDE))
    factor = rows[0:MOSTE, QUARTER:QUARTER + 1] + rows[0:MOSTE, QUARTER + 1:QUARTER + 2]
    xs[...] = jnp.zeros(xs.shape, F32)
    for j in range(4):
        low = QUARTER * j // 128 * 128
        features = jnp.where(
            iota((MOSTE, WIDE), 1) < QUARTER, rows[MOSTE * j:MOSTE * (j + 1)], 0.0
        )
        features = jnp.concatenate([features, jnp.zeros((MOSTE, 128), F32)], axis=1)
        if QUARTER * j - low:
            features = pltpu.roll(features, QUARTER * j - low, 1)
        xs[:, low:low + WIDE + 128] += features
    features = xs[:, :D].astype(BF16)
    gate = dot(features, wg_ref[...], ((1,), (1,))) * factor
    up = dot(features, wu_ref[...], ((1,), (1,))) * factor
    activation = (gate * jax.nn.sigmoid(1.702 * gate) * (up + 1.0)).astype(BF16)
    oflat[:, PADDED - 128:] = jnp.zeros((MOSTE, 128), F32)
    oflat[:, :D] = dot(activation, wd_ref[...]) * slot_weight
    for k in range(KV):
        esend[k] = window(oflat, k).astype(BF16)
    finish([
        start(esend.at[lax.rem(kv + d, KV)], erecv.at[d - 1], to_kv[d - 1])
        for d in range(1, KV)
    ])
    summed = esend[kv].astype(F32)
    for d in range(KV - 1):
        summed = summed + erecv[d].astype(F32)

    dense = dot(back, summed.astype(BF16), ((0,), (0,)))
    dn[...] = dense.astype(BF16).reshape(dn.shape)

    def fold_half(i, h):
        finish([start(dn.at[h, 1 - c], r1.at[i], to_core)])
        total = dn[h, c].astype(F32) + r1[i].astype(F32)
        for xx in range(NX):
            for yy in range(NY):
                low = 4 * (NY * xx + yy)
                e1[i, xx, yy] = total[low:low + 4]
        finish([
            start(e1.at[i, xx, yy], rx2.at[i, k], to_plane[k])
            for k, (xx, yy) in enumerate(in_plane)
        ])
        total = e1[i, x, y]
        for k in range(len(others)):
            total = total + rx2[i, k]
        e3[i] = total

    fold_half(1, far)
    across = [start(e3.at[1], rz2, to_z)]
    fold_half(0, z)
    finish(across)
    out = residual_sum + e3[0] + rz2[...]
    out_ref[...] = out[:, 0:SLICE].astype(BF16)


def on_device(
    queries, prompt_cache, gen_cache, gen_lengths, new_kv, w_out, residual, norm_gain,
    w_gate, w_up, w_down, expert_ids, route_weights,
):
    ffe = w_gate.shape[2]
    anywhere = pl.BlockSpec(memory_space=pl.ANY)
    vmem = pl.BlockSpec(memory_space=pltpu.VMEM)
    smem = pl.BlockSpec(memory_space=pltpu.SMEM)
    grid = (NZ, NC, NX, NY)
    scratch = [
        pltpu.VMEM(prompt_cache.shape, BF16),
        pltpu.VMEM(gen_cache.shape[1:], BF16),
        pltpu.VMEM((D, 256), BF16),
        pltpu.VMEM((ffe, D), BF16),
        pltpu.VMEM((ffe, D), BF16),
        pltpu.VMEM((ffe, D), BF16),
        pltpu.VMEM((16, 256), F32),
        pltpu.VMEM((16, 128), F32),
        pltpu.VMEM((8, LANES), F32),
        pltpu.VMEM((1, LANES), F32),
        pltpu.VMEM((16, 64), F32),
        pltpu.VMEM(grid + (16, 128), BF16),
        pltpu.VMEM(grid + (16, 128), F32),
        pltpu.VMEM((2, NX, NY, 16, 128), F32),
        pltpu.VMEM((2, NX, NY, 16, 128), F32),
        pltpu.VMEM((2, NX * NY - 1, 16, 128), F32),
        pltpu.VMEM((2, 16, 128), F32),
        pltpu.VMEM((16, 128), F32),
        pltpu.VMEM((8, PADDED), F32),
        pltpu.VMEM((KV, 4, LANES), BF16),
        pltpu.VMEM((KV - 1, 4, LANES), BF16),
        pltpu.VMEM((NZ * KV, 4, LANES), BF16),
        pltpu.VMEM((32, WIDE), F32),
        pltpu.VMEM(grid + (16, WIDE), BF16),
        pltpu.VMEM((4 * MOSTE, 1024), BF16),
        pltpu.VMEM((MOSTE, PADDED), F32),
        pltpu.VMEM((MOSTE, PADDED), F32),
        pltpu.VMEM((KV, MOSTE, LANES), BF16),
        pltpu.VMEM((KV - 1, MOSTE, LANES), BF16),
        pltpu.VMEM((NZ, NC, 64, LANES), BF16),
        pltpu.VMEM((2, 64, LANES), BF16),
        pltpu.VMEM((2, NX, NY, 4, LANES), F32),
        pltpu.VMEM((2, NX * NY - 1, 4, LANES), F32),
        pltpu.VMEM((2, 4, LANES), F32),
        pltpu.VMEM((4, LANES), F32),
        pltpu.SemaphoreType.DMA((160,)),
        pltpu.SemaphoreType.DMA((160,)),
        pltpu.SemaphoreType.DMA((6,)),
    ]
    out = pl.pallas_call(
        kernel,
        out_shape=jax.ShapeDtypeStruct(residual.shape[1:], BF16),
        in_specs=[vmem, anywhere, anywhere, vmem, smem, anywhere, vmem, vmem]
        + [anywhere] * 3 + [vmem] * 2,
        out_specs=vmem,
        scratch_shapes=scratch,
        compiler_params=pltpu.CompilerParams(
            collective_id=0, has_side_effects=True, vmem_limit_bytes=60 * 1024 * 1024
        ),
        name="layer",
    )(
        queries[0], prompt_cache, gen_cache[0], new_kv[0], gen_lengths, w_out.T, residual[0],
        norm_gain.reshape(1, SLICE), w_gate[0].T, w_up[0].T, w_down[0],
        expert_ids.transpose(1, 2, 0), route_weights.transpose(1, 2, 0),
    )
    return out[None]


def solution(mesh):
    in_specs = (
        P("roll", None, "kv"),
        P(None, "roll", "kv"),
        P("roll", None, "kv"),
        P("roll"),
        P("roll", None, "kv"),
        P("kv", None),
        P("roll", None, "kv"),
        P("kv"),
        P("roll", None, "kv"),
        P("roll", None, "kv"),
        P("roll", "kv", None),
        P(),
        P(),
    )
    out_specs = P("roll", None, "kv")
    return jax.shard_map(
        on_device, mesh=mesh, in_specs=in_specs, out_specs=out_specs, check_vma=False
    )
```

```python
import jax
import jax.numpy as jnp
from jax import lax
from jax.experimental import pallas as pl
from jax.experimental.pallas import tpu as pltpu
from jax.sharding import PartitionSpec as P

D = 2880
HEAD = 64
MOSTE = 48
KV = 8
NX, NZ, NY, NC = 4, 2, 4, 2
SLICE = D // KV
LANES = 384
QUARTER = 720
WIDE = 768
PADDED = 2944
F32 = jnp.float32
BF16 = jnp.bfloat16
MESH = pl.DeviceIdType.MESH


def iota(shape, axis):
    return lax.broadcasted_iota(jnp.int32, shape, axis)


def onehot(mask):
    return jnp.where(mask, 1.0, 0.0).astype(BF16)


def dot(a, b, dims=((1,), (0,))):
    return lax.dot_general(a, b, (dims, ((), ())), preferred_element_type=F32)


def packed(m, l, acc):
    lane = iota(acc.shape, 1)
    return jnp.where(lane == 0, m, jnp.where(lane == 1, l, jnp.where(lane >= HEAD, acc, 0.0)))


def merge(rows):
    top = rows[0][:, 0:1]
    for r in rows[1:]:
        top = jnp.maximum(top, r[:, 0:1])
    total = rows[0] * jnp.exp(rows[0][:, 0:1] - top)
    for r in rows[1:]:
        total = total + r * jnp.exp(r[:, 0:1] - top)
    return jnp.where(iota(total.shape, 1) == 0, top, total)


def window(ref, k):
    start = SLICE * k // 128 * 128
    wide = ref[:, start:start + 512]
    shift = SLICE * k - start
    if shift:
        wide = pltpu.roll(wide, 512 - shift, 1)
    return wide[:, :LANES]


def kernel(
    q_ref, prompt_hbm, gen_hbm, new_ref, len_ref, wout_hbm, res_ref, gain_ref,
    wg_hbm, wu_hbm, wd_hbm, ids_ref, rw_ref, out_ref,
    prompt_ref, gen_ref, wout_ref, wg_ref, wu_ref, wd_ref,
    padq, padn, padr, padg, pres,
    qbuf, part, rc, s1, rx, s3, rz,
    proj, rsend, rrecv, agbuf, blk, ybuf, choose, xs,
    oflat, esend, erecv, dn, r1, e1, rx2, e3, rz2,
    send_sem, recv_sem, load_sem,
):
    roll = lax.axis_index("roll")
    kv = lax.axis_index("kv")
    c = lax.rem(roll, NC)
    y = lax.rem(roll // NC, NY)
    z = lax.rem(roll // (NC * NY), NZ)
    x = roll // (NC * NY * NZ)

    def at(xx, zz, yy, cc):
        return (((xx * NZ + zz) * NY + yy) * NC + cc, kv)

    to_core = at(x, z, y, 1 - c)
    to_z = at(x, 1 - z, y, c)
    to_x = [at(lax.rem(x + d, NX), z, y, c) for d in range(1, NX)]
    to_y = [at(x, z, lax.rem(y + d, NY), c) for d in range(1, NY)]
    others = [(dx, dy) for dx in range(NX) for dy in range(NY) if dx or dy]
    others.sort(key=lambda d: -min(d[0], NX - d[0]) - min(d[1], NY - d[1]))
    in_plane = [(lax.rem(x + dx, NX), lax.rem(y + dy, NY)) for dx, dy in others]
    to_plane = [at(xx, z, yy, c) for xx, yy in in_plane]
    bits = [lax.rem(kv, 2), lax.rem(kv // 2, 2), kv // 4]
    peers = [
        sum((1 - bit if m >> i & 1 else bit) * (1 << i) for i, bit in enumerate(bits))
        for m in (7, 6, 5, 4, 3, 2, 1)
    ]
    to_kv = [(roll, peer) for peer in peers]
    column = z * KV + kv
    to_column = []
    for d in sorted(range(1, NZ * KV), key=lambda d: abs(d - KV)):
        there = lax.rem(column + d, NZ * KV)
        to_column.append((at(x, there // KV, y, c)[0], lax.rem(there, KV)))
    partners = [to_core] + to_plane + to_column
    barrier = pltpu.get_barrier_semaphore()
    for device in partners:
        pl.semaphore_signal(barrier, inc=1, device_id=device, device_id_type=MESH)

    loads = [
        pltpu.make_async_copy(src, dst, load_sem.at[i])
        for i, (src, dst) in enumerate([
            (gen_hbm, gen_ref), (prompt_hbm, prompt_ref), (wout_hbm, wout_ref),
            (wg_hbm, wg_ref), (wu_hbm, wu_ref), (wd_hbm, wd_ref),
        ])
    ]
    for load in loads:
        load.start()

    next_sem = [0]

    def start(src, dst, device):
        i = next_sem[0]
        next_sem[0] += 1
        copy = pltpu.make_async_remote_copy(
            src_ref=src, dst_ref=dst, send_sem=send_sem.at[i], recv_sem=recv_sem.at[i],
            device_id=device, device_id_type=MESH,
        )
        copy.start()
        return copy

    def finish(copies):
        for copy in copies:
            copy.wait()

    padq[...] = jnp.zeros((16, 256), F32)
    padq[0:4, :] = q_ref[...].astype(F32) * 0.125
    row, col = iota((128, 256), 0), iota((128, 256), 1)
    own_head = (iota((16, 256), 0) >> 2) == (iota((16, 256), 1) >> 6)
    each = dot(onehot((iota((16, 16), 0) & 3) == iota((16, 16), 1)), padq[...].astype(BF16))
    each = jnp.where(own_head, each, 0.0).astype(BF16)
    fold = onehot((row < HEAD) & ((col & (HEAD - 1)) == row))
    own = dot(each, fold, ((1,), (1,))).astype(BF16)
    qbuf[z, c, x, y] = own

    pres[...] = jnp.zeros((16, 64), F32)
    weights = []
    for t in range(4):
        match = ids_ref[t] == roll
        pres[t:t + 1, :] = jnp.max(jnp.where(match, 1.0, 0.0), axis=0, keepdims=True)
        weights.append(jnp.sum(jnp.where(match, rw_ref[t], 0.0), axis=0, keepdims=True))
    present = pres[...]
    upto = onehot(iota((64, 64), 0) <= iota((64, 64), 1))
    earlier = onehot(iota((16, 16), 1) < iota((16, 16), 0))
    totals = jnp.broadcast_to(jnp.sum(present, axis=1, keepdims=True), (16, 64))
    slot = dot(present.astype(BF16), upto) + dot(earlier, totals.astype(BF16)) - 1.0
    slot = jnp.where(present > 0.5, slot, -1.0)
    slot_half = slot.astype(BF16)

    def place(sample):
        return (
            (((sample >> 3) & 1) << 5) | ((sample & 1) << 4)
            | ((sample >> 4) << 2) | ((sample >> 1) & 3)
        )

    padr[...] = jnp.zeros((8, LANES), F32)
    padr[0:4, 0:SLICE] = res_ref[...].astype(F32)
    padg[...] = jnp.zeros((1, LANES), F32)
    padg[:, 0:SLICE] = gain_ref[...].reshape(1, SLICE)
    pl.semaphore_wait(barrier, len(partners))

    def attend(h):
        scores = []
        for xx in range(NX):
            q = jnp.concatenate([qbuf[h, cc, xx].reshape(64, 128) for cc in range(NC)], axis=0)
            scores.append(dot(q, prompt_ref[xx], ((1,), (1,))))
        tops = [jnp.max(s, axis=1, keepdims=True) for s in scores]
        scores = [jnp.exp(s - m) for s, m in zip(scores, tops)]
        totals = [jnp.sum(w, axis=1, keepdims=True) for w in scores]
        for xx in range(NX):
            values = dot(scores[xx].astype(BF16), prompt_ref[xx])
            rows = packed(tops[xx], totals[xx], values)
            for cc in range(NC):
                part[h, cc, xx] = rows[64 * cc:64 * (cc + 1)].reshape(NY, 16, 128)

    def share_plane(h):
        return [start(qbuf.at[h, c, x, y], qbuf.at[h, c, x, y], device) for device in to_plane]

    def share_core(h):
        return [start(qbuf.at[h, c], qbuf.at[h, c], to_core)]

    def sum_core(i, h):
        return [start(part.at[h, 1 - c], rc.at[i], to_core)]

    def add_core(i, h):
        rows = (NX * NY * 16, 128)
        s1[i] = merge([part[h, c].reshape(rows), rc[i].reshape(rows)]).reshape(s1.shape[1:])

    def sum_plane(i):
        return [
            start(s1.at[i, xx, yy], rx.at[i, k], to_plane[k])
            for k, (xx, yy) in enumerate(in_plane)
        ]

    def add_plane(i):
        s3[i] = merge([s1[i, x, y]] + [rx[i, k] for k in range(len(others))])

    far = 1 - z
    across = [start(qbuf.at[z, c, x, y], qbuf.at[z, c, x, y], to_z)]
    flight = share_plane(z)
    padn[...] = jnp.zeros((16, 128), F32)
    padn[0:4, :] = new_ref[...].astype(F32)
    fresh = padn[...].astype(BF16)
    loads[0].wait()
    live = iota((16, 128), 1) < len_ref[0]
    gen_s = jnp.where(live, dot(own, gen_ref[...], ((1,), (1,))), -1e30)
    causal = iota((16, 16), 1) <= (iota((16, 16), 0) & 3)
    new_s = jnp.where(causal, dot(own, fresh, ((1,), (1,))), -1e30)
    top = jnp.maximum(
        jnp.max(gen_s, axis=1, keepdims=True), jnp.max(new_s, axis=1, keepdims=True)
    )
    gen_w = jnp.exp(gen_s - top)
    new_w = jnp.exp(new_s - top)
    own_part = packed(
        top,
        jnp.sum(gen_w, axis=1, keepdims=True) + jnp.sum(new_w, axis=1, keepdims=True),
        dot(gen_w.astype(BF16), gen_ref[...]) + dot(new_w.astype(BF16), fresh),
    )
    finish(flight)
    finish(share_core(z))
    finish(across)
    flight = share_plane(far)
    loads[1].wait()
    attend(z)
    part[z, c, x, y] = merge([part[z, c, x, y], own_part])
    near = sum_core(0, z)
    finish(flight)
    flight = share_core(far)
    finish(near)
    add_core(0, z)
    near = sum_plane(0)
    finish(flight)
    attend(far)
    flight = sum_core(1, far)
    finish(near)
    add_plane(0)
    finish(flight)
    add_core(1, far)
    finish(sum_plane(1))
    add_plane(1)
    flight = [start(s3.at[1], rz, to_z)]
    spread = onehot(place(iota((64, 1024), 0)) == (iota((64, 1024), 1) >> 4))
    wide = dot(slot_half, spread)
    wide = jnp.where(iota((16, 1024), 0) == (iota((16, 1024), 1) & 3), wide, 0.0)
    wide = jnp.sum(wide, axis=0, keepdims=True)
    lane = iota((1, 1024), 1)
    code = jnp.where(wide < -0.5, -1.0, wide + MOSTE * ((lane >> 2) & 3).astype(F32))
    choose[...] = onehot(iota((4 * MOSTE, 1024), 0) == code.astype(jnp.int32))
    spread = onehot(place(iota((64, 256), 0)) == (iota((64, 256), 1) >> 2))
    wide = dot(slot_half, spread)
    wide = jnp.where(iota((16, 256), 0) == (iota((16, 256), 1) & 3), wide, 0.0)
    wide = jnp.sum(wide, axis=0, keepdims=True).astype(jnp.int32)
    back = onehot(iota((MOSTE, 256), 0) == wide)
    slot_weight = jnp.zeros((MOSTE, 1), F32)
    slot_whole = slot.astype(jnp.int32)
    for t in range(4):
        mine = iota((MOSTE, 64), 0) == slot_whole[t:t + 1]
        slot_weight = slot_weight + jnp.sum(
            jnp.where(mine, weights[t], 0.0), axis=1, keepdims=True
        )
    finish(flight)
    final = merge([s3[0], rz[...]])
    lane = iota((16, 128), 1)
    attended = jnp.where(lane >= HEAD, final / final[:, 1:2], 0.0).astype(BF16)

    row, col = iota((128, 256), 0), iota((128, 256), 1)
    copies = onehot((row >= HEAD) & ((col & (HEAD - 1)) == row - HEAD))
    heads = jnp.where(own_head, dot(attended, copies), 0.0)
    steps = onehot((iota((16, 16), 1) & 3) == iota((16, 16), 0))
    attended = dot(steps, heads.astype(BF16)).astype(BF16)
    proj[:, PADDED - 128:] = jnp.zeros((8, 128), F32)
    loads[2].wait()
    proj[:, :D] = dot(attended, wout_ref[...], ((1,), (1,)))[0:8]
    for k in range(KV):
        rsend[k] = window(proj, k)[0:4].astype(BF16)
    finish([
        start(rsend.at[peer], rrecv.at[k], to_kv[k]) for k, peer in enumerate(peers)
    ])
    projected = rsend[kv].astype(F32)
    for d in range(KV - 1):
        projected = projected + rrecv[d].astype(F32)
    lane = iota((4, LANES), 1)
    residual_sum = jnp.where(lane < SLICE, padr[0:4, :] + projected, 0.0)

    squares = jnp.sum(residual_sum * residual_sum, axis=1, keepdims=True)
    high = squares.astype(BF16).astype(F32)
    scaled = residual_sum * padg[...]
    agbuf[column] = jnp.where(
        lane == SLICE, high, jnp.where(lane == SLICE + 1, squares - high, scaled)
    ).astype(BF16)
    finish([start(agbuf.at[column], agbuf.at[column], device) for device in to_column])
    for zz in range(NZ):
        pieces = [agbuf[KV * zz + k].astype(F32) for k in range(KV)]
        squares = jnp.zeros((4, 1), F32)
        for piece in pieces:
            squares = squares + piece[:, SLICE:SLICE + 1] + piece[:, SLICE + 1:SLICE + 2]
        inverse = lax.rsqrt(squares / D + 1e-05)
        high = inverse.astype(BF16).astype(F32)
        for k, piece in enumerate(pieces):
            piece = jnp.where(
                lane == SLICE, high, jnp.where(lane == SLICE + 1, inverse - high, piece)
            )
            low, half = 16 * zz + 4 * (k // 2), LANES * (k % 2)
            blk[low:low + 4, half:half + LANES] = piece
    block = blk[...]
    block = jnp.where(
        iota(block.shape, 1) < SLICE, block, pltpu.roll(block, WIDE - (LANES - SLICE), 1)
    ).astype(BF16)
    ybuf[0, c, x, y] = block[0:16]
    ybuf[1, c, x, y] = block[16:32]

    a = [start(ybuf.at[0, c, x, y], ybuf.at[0, c, x, y], device) for device in to_y]
    b = [start(ybuf.at[1, c, x, y], ybuf.at[1, c, x, y], device) for device in to_x]
    finish(a)
    a = [start(ybuf.at[0, c, x], ybuf.at[0, c, x], device) for device in to_x]
    cores = [start(ybuf.at[0, c, x], ybuf.at[0, c, x], to_core)]
    finish(b)
    b = [start(ybuf.at[1, c, :, y], ybuf.at[1, c, :, y], device) for device in to_y]
    cores.append(start(ybuf.at[1, c, :, y], ybuf.at[1, c, :, y], to_core))
    for d in (1, 3, 2):
        a[d - 1].wait()
        xx = lax.rem(x + NX - d, NX)
        cores.append(start(ybuf.at[0, c, xx], ybuf.at[0, c, xx], to_core))
        b[d - 1].wait()
        yy = lax.rem(y + NY - d, NY)
        cores.append(start(ybuf.at[1, c, :, yy], ybuf.at[1, c, :, yy], to_core))
    for load in loads[3:]:
        load.wait()
    finish(cores)

    rows = dot(choose[...], ybuf[...].reshape(1024, WIDE))
    factor = rows[0:MOSTE, QUARTER:QUARTER + 1] + rows[0:MOSTE, QUARTER + 1:QUARTER + 2]
    xs[...] = jnp.zeros(xs.shape, F32)
    for j in range(4):
        low = QUARTER * j // 128 * 128
        features = jnp.where(
            iota((MOSTE, WIDE), 1) < QUARTER, rows[MOSTE * j:MOSTE * (j + 1)], 0.0
        )
        features = jnp.concatenate([features, jnp.zeros((MOSTE, 128), F32)], axis=1)
        if QUARTER * j - low:
            features = pltpu.roll(features, QUARTER * j - low, 1)
        xs[:, low:low + WIDE + 128] += features
    features = xs[:, :D].astype(BF16)
    gate = dot(features, wg_ref[...], ((1,), (1,))) * factor
    up = dot(features, wu_ref[...], ((1,), (1,))) * factor
    activation = (gate * jax.nn.sigmoid(1.702 * gate) * (up + 1.0)).astype(BF16)
    oflat[:, PADDED - 128:] = jnp.zeros((MOSTE, 128), F32)
    oflat[:, :D] = dot(activation, wd_ref[...]) * slot_weight
    for k in range(KV):
        esend[k] = window(oflat, k).astype(BF16)
    finish([
        start(esend.at[peer], erecv.at[k], to_kv[k]) for k, peer in enumerate(peers)
    ])
    summed = esend[kv].astype(F32)
    for d in range(KV - 1):
        summed = summed + erecv[d].astype(F32)

    dense = dot(back, summed.astype(BF16), ((0,), (0,)))
    dn[...] = dense.astype(BF16).reshape(dn.shape)

    def fold_half(i, h):
        finish([start(dn.at[h, 1 - c], r1.at[i], to_core)])
        total = dn[h, c].astype(F32) + r1[i].astype(F32)
        for xx in range(NX):
            for yy in range(NY):
                low = 4 * (NY * xx + yy)
                e1[i, xx, yy] = total[low:low + 4]
        finish([
            start(e1.at[i, xx, yy], rx2.at[i, k], to_plane[k])
            for k, (xx, yy) in enumerate(in_plane)
        ])
        total = e1[i, x, y]
        for k in range(len(others)):
            total = total + rx2[i, k]
        e3[i] = total

    fold_half(1, far)
    across = [start(e3.at[1], rz2, to_z)]
    fold_half(0, z)
    finish(across)
    out = residual_sum + e3[0] + rz2[...]
    out_ref[...] = out[:, 0:SLICE].astype(BF16)


def on_device(
    queries, prompt_cache, gen_cache, gen_lengths, new_kv, w_out, residual, norm_gain,
    w_gate, w_up, w_down, expert_ids, route_weights,
):
    ffe = w_gate.shape[2]
    anywhere = pl.BlockSpec(memory_space=pl.ANY)
    vmem = pl.BlockSpec(memory_space=pltpu.VMEM)
    smem = pl.BlockSpec(memory_space=pltpu.SMEM)
    grid = (NZ, NC, NX, NY)
    scratch = [
        pltpu.VMEM(prompt_cache.shape, BF16),
        pltpu.VMEM(gen_cache.shape[1:], BF16),
        pltpu.VMEM((D, 256), BF16),
        pltpu.VMEM((ffe, D), BF16),
        pltpu.VMEM((ffe, D), BF16),
        pltpu.VMEM((ffe, D), BF16),
        pltpu.VMEM((16, 256), F32),
        pltpu.VMEM((16, 128), F32),
        pltpu.VMEM((8, LANES), F32),
        pltpu.VMEM((1, LANES), F32),
        pltpu.VMEM((16, 64), F32),
        pltpu.VMEM(grid + (16, 128), BF16),
        pltpu.VMEM(grid + (16, 128), F32),
        pltpu.VMEM((2, NX, NY, 16, 128), F32),
        pltpu.VMEM((2, NX, NY, 16, 128), F32),
        pltpu.VMEM((2, NX * NY - 1, 16, 128), F32),
        pltpu.VMEM((2, 16, 128), F32),
        pltpu.VMEM((16, 128), F32),
        pltpu.VMEM((8, PADDED), F32),
        pltpu.VMEM((KV, 4, LANES), BF16),
        pltpu.VMEM((KV - 1, 4, LANES), BF16),
        pltpu.VMEM((NZ * KV, 4, LANES), BF16),
        pltpu.VMEM((32, WIDE), F32),
        pltpu.VMEM(grid + (16, WIDE), BF16),
        pltpu.VMEM((4 * MOSTE, 1024), BF16),
        pltpu.VMEM((MOSTE, PADDED), F32),
        pltpu.VMEM((MOSTE, PADDED), F32),
        pltpu.VMEM((KV, MOSTE, LANES), BF16),
        pltpu.VMEM((KV - 1, MOSTE, LANES), BF16),
        pltpu.VMEM((NZ, NC, 64, LANES), BF16),
        pltpu.VMEM((2, 64, LANES), BF16),
        pltpu.VMEM((2, NX, NY, 4, LANES), F32),
        pltpu.VMEM((2, NX * NY - 1, 4, LANES), F32),
        pltpu.VMEM((2, 4, LANES), F32),
        pltpu.VMEM((4, LANES), F32),
        pltpu.SemaphoreType.DMA((160,)),
        pltpu.SemaphoreType.DMA((160,)),
        pltpu.SemaphoreType.DMA((6,)),
    ]
    out = pl.pallas_call(
        kernel,
        out_shape=jax.ShapeDtypeStruct(residual.shape[1:], BF16),
        in_specs=[vmem, anywhere, anywhere, vmem, smem, anywhere, vmem, vmem]
        + [anywhere] * 3 + [vmem] * 2,
        out_specs=vmem,
        scratch_shapes=scratch,
        compiler_params=pltpu.CompilerParams(
            collective_id=0, has_side_effects=True, vmem_limit_bytes=60 * 1024 * 1024
        ),
        name="layer",
    )(
        queries[0], prompt_cache, gen_cache[0], new_kv[0], gen_lengths, w_out.T, residual[0],
        norm_gain, w_gate[0].T, w_up[0].T, w_down[0],
        expert_ids.transpose(1, 2, 0), route_weights.transpose(1, 2, 0),
    )
    return out[None]


def solution(mesh):
    in_specs = (
        P("roll", None, "kv"),
        P(None, "roll", "kv"),
        P("roll", None, "kv"),
        P("roll"),
        P("roll", None, "kv"),
        P("kv", None),
        P("roll", None, "kv"),
        P("kv"),
        P("roll", None, "kv"),
        P("roll", None, "kv"),
        P("roll", "kv", None),
        P(),
        P(),
    )
    out_specs = P("roll", None, "kv")
    return jax.shard_map(
        on_device, mesh=mesh, in_specs=in_specs, out_specs=out_specs, check_vma=False
    )
```

```python
import jax
import jax.numpy as jnp
from jax import lax
from jax.experimental import pallas as pl
from jax.experimental.pallas import tpu as pltpu
from jax.sharding import PartitionSpec as P

D = 2880
HEAD = 64
MOSTE = 48
KV = 8
NX, NZ, NY, NC = 4, 2, 4, 2
SLICE = D // KV
LANES = 384
QUARTER = 720
WIDE = 768
PADDED = 2944
F32 = jnp.float32
BF16 = jnp.bfloat16
MESH = pl.DeviceIdType.MESH


def iota(shape, axis):
    return lax.broadcasted_iota(jnp.int32, shape, axis)


def onehot(mask):
    return jnp.where(mask, 1.0, 0.0).astype(BF16)


def dot(a, b, dims=((1,), (0,))):
    return lax.dot_general(a, b, (dims, ((), ())), preferred_element_type=F32)


def packed(m, l, acc):
    lane = iota(acc.shape, 1)
    high = l.astype(BF16).astype(F32)
    acc = jnp.where(lane >= HEAD, acc, 0.0)
    return jnp.where(lane == 0, m, jnp.where(lane == 1, high, jnp.where(lane == 2, l - high, acc)))


def merge(rows):
    rows = [r.astype(F32) for r in rows]
    top = rows[0][:, 0:1]
    for r in rows[1:]:
        top = jnp.maximum(top, r[:, 0:1])
    total = rows[0] * jnp.exp(rows[0][:, 0:1] - top)
    for r in rows[1:]:
        total = total + r * jnp.exp(r[:, 0:1] - top)
    return packed(top, total[:, 1:2] + total[:, 2:3], total)


def window(ref, k):
    start = SLICE * k // 128 * 128
    wide = ref[:, start:start + 512]
    shift = SLICE * k - start
    if shift:
        wide = pltpu.roll(wide, 512 - shift, 1)
    return wide[:, :LANES]


def kernel(
    q_ref, prompt_hbm, gen_hbm, new_ref, len_ref, wout_hbm, res_ref, gain_ref,
    wg_hbm, wu_hbm, wd_hbm, ids_ref, rw_ref, out_ref,
    prompt_ref, gen_ref, wout_ref, wg_ref, wu_ref, wd_ref,
    padq, padn, padr, padg, pres,
    qbuf, part, rc, s1, rx, s3, rz,
    proj, rsend, rrecv, agbuf, blk, ybuf, choose, xs,
    oflat, esend, erecv, dn, r1, e1, rx2, e3, rz2,
    send_sem, recv_sem, load_sem,
):
    roll = lax.axis_index("roll")
    kv = lax.axis_index("kv")
    c = lax.rem(roll, NC)
    y = lax.rem(roll // NC, NY)
    z = lax.rem(roll // (NC * NY), NZ)
    x = roll // (NC * NY * NZ)

    def at(xx, zz, yy, cc):
        return (((xx * NZ + zz) * NY + yy) * NC + cc, kv)

    to_core = at(x, z, y, 1 - c)
    to_z = at(x, 1 - z, y, c)
    to_x = [at(lax.rem(x + d, NX), z, y, c) for d in range(1, NX)]
    to_y = [at(x, z, lax.rem(y + d, NY), c) for d in range(1, NY)]
    others = [(dx, dy) for dx in range(NX) for dy in range(NY) if dx or dy]
    others.sort(key=lambda d: -min(d[0], NX - d[0]) - min(d[1], NY - d[1]))
    in_plane = [(lax.rem(x + dx, NX), lax.rem(y + dy, NY)) for dx, dy in others]
    to_plane = [at(xx, z, yy, c) for xx, yy in in_plane]
    bits = [lax.rem(kv, 2), lax.rem(kv // 2, 2), kv // 4]
    peers = [
        sum((1 - bit if m >> i & 1 else bit) * (1 << i) for i, bit in enumerate(bits))
        for m in (7, 6, 5, 4, 3, 2, 1)
    ]
    to_kv = [(roll, peer) for peer in peers]
    column = z * KV + kv
    to_column = []
    for d in sorted(range(1, NZ * KV), key=lambda d: abs(d - KV)):
        there = lax.rem(column + d, NZ * KV)
        to_column.append((at(x, there // KV, y, c)[0], lax.rem(there, KV)))
    partners = [to_core] + to_plane + to_column
    barrier = pltpu.get_barrier_semaphore()
    for device in partners:
        pl.semaphore_signal(barrier, inc=1, device_id=device, device_id_type=MESH)

    loads = [
        pltpu.make_async_copy(src, dst, load_sem.at[i])
        for i, (src, dst) in enumerate([
            (gen_hbm, gen_ref), (prompt_hbm, prompt_ref), (wout_hbm, wout_ref),
            (wg_hbm, wg_ref), (wu_hbm, wu_ref), (wd_hbm, wd_ref),
        ])
    ]
    for load in loads:
        load.start()

    next_sem = [0]

    def start(src, dst, device):
        i = next_sem[0]
        next_sem[0] += 1
        copy = pltpu.make_async_remote_copy(
            src_ref=src, dst_ref=dst, send_sem=send_sem.at[i], recv_sem=recv_sem.at[i],
            device_id=device, device_id_type=MESH,
        )
        copy.start()
        return copy

    def finish(copies):
        for copy in copies:
            copy.wait()

    padq[...] = jnp.zeros((16, 256), F32)
    padq[0:4, :] = q_ref[...].astype(F32) * 0.125
    row, col = iota((128, 256), 0), iota((128, 256), 1)
    own_head = (iota((16, 256), 0) >> 2) == (iota((16, 256), 1) >> 6)
    each = dot(onehot((iota((16, 16), 0) & 3) == iota((16, 16), 1)), padq[...].astype(BF16))
    each = jnp.where(own_head, each, 0.0).astype(BF16)
    fold = onehot((row < HEAD) & ((col & (HEAD - 1)) == row))
    own = dot(each, fold, ((1,), (1,))).astype(BF16)
    qbuf[z, c, x, y] = own

    pres[...] = jnp.zeros((16, 64), F32)
    weights = []
    for t in range(4):
        match = ids_ref[t] == roll
        pres[t:t + 1, :] = jnp.max(jnp.where(match, 1.0, 0.0), axis=0, keepdims=True)
        weights.append(jnp.sum(jnp.where(match, rw_ref[t], 0.0), axis=0, keepdims=True))
    present = pres[...]
    upto = onehot(iota((64, 64), 0) <= iota((64, 64), 1))
    earlier = onehot(iota((16, 16), 1) < iota((16, 16), 0))
    totals = jnp.broadcast_to(jnp.sum(present, axis=1, keepdims=True), (16, 64))
    slot = dot(present.astype(BF16), upto) + dot(earlier, totals.astype(BF16)) - 1.0
    slot = jnp.where(present > 0.5, slot, -1.0)
    slot_half = slot.astype(BF16)

    def place(sample):
        return (
            (((sample >> 3) & 1) << 5) | ((sample & 1) << 4)
            | ((sample >> 4) << 2) | ((sample >> 1) & 3)
        )

    padr[...] = jnp.zeros((8, LANES), F32)
    padr[0:4, 0:SLICE] = res_ref[...].astype(F32)
    padg[...] = jnp.zeros((1, LANES), F32)
    padg[:, 0:SLICE] = gain_ref[...].reshape(1, SLICE)
    pl.semaphore_wait(barrier, len(partners))

    def attend(h):
        scores = []
        for xx in range(NX):
            q = jnp.concatenate([qbuf[h, cc, xx].reshape(64, 128) for cc in range(NC)], axis=0)
            scores.append(dot(q, prompt_ref[xx], ((1,), (1,))))
        tops = [jnp.max(s, axis=1, keepdims=True).astype(BF16).astype(F32) for s in scores]
        scores = [jnp.exp(s - m) for s, m in zip(scores, tops)]
        totals = [jnp.sum(w, axis=1, keepdims=True) for w in scores]
        for xx in range(NX):
            values = dot(scores[xx].astype(BF16), prompt_ref[xx])
            rows = packed(tops[xx], totals[xx], values).astype(BF16)
            for cc in range(NC):
                part[h, cc, xx] = rows[64 * cc:64 * (cc + 1)].reshape(NY, 16, 128)

    def share_plane(h):
        return [start(qbuf.at[h, c, x, y], qbuf.at[h, c, x, y], device) for device in to_plane]

    def share_core(h):
        return [start(qbuf.at[h, c], qbuf.at[h, c], to_core)]

    def sum_core(i, h):
        return [start(part.at[h, 1 - c], rc.at[i], to_core)]

    def add_core(i, h):
        rows = (NX * NY * 16, 128)
        total = merge([part[h, c].reshape(rows), rc[i].reshape(rows)])
        s1[i] = total.astype(BF16).reshape(s1.shape[1:])

    def sum_plane(i):
        return [
            start(s1.at[i, xx, yy], rx.at[i, k], to_plane[k])
            for k, (xx, yy) in enumerate(in_plane)
        ]

    def add_plane(i):
        s3[i] = merge([s1[i, x, y]] + [rx[i, k] for k in range(len(others))])

    far = 1 - z
    across = [start(qbuf.at[z, c, x, y], qbuf.at[z, c, x, y], to_z)]
    flight = share_plane(z)
    padn[...] = jnp.zeros((16, 128), F32)
    padn[0:4, :] = new_ref[...].astype(F32)
    fresh = padn[...].astype(BF16)
    loads[0].wait()
    live = iota((16, 128), 1) < len_ref[0]
    gen_s = jnp.where(live, dot(own, gen_ref[...], ((1,), (1,))), -1e30)
    causal = iota((16, 16), 1) <= (iota((16, 16), 0) & 3)
    new_s = jnp.where(causal, dot(own, fresh, ((1,), (1,))), -1e30)
    top = jnp.maximum(
        jnp.max(gen_s, axis=1, keepdims=True), jnp.max(new_s, axis=1, keepdims=True)
    ).astype(BF16).astype(F32)
    gen_w = jnp.exp(gen_s - top)
    new_w = jnp.exp(new_s - top)
    own_part = packed(
        top,
        jnp.sum(gen_w, axis=1, keepdims=True) + jnp.sum(new_w, axis=1, keepdims=True),
        dot(gen_w.astype(BF16), gen_ref[...]) + dot(new_w.astype(BF16), fresh),
    )
    finish(flight)
    finish(share_core(z))
    finish(across)
    flight = share_plane(far)
    loads[1].wait()
    attend(z)
    part[z, c, x, y] = merge([part[z, c, x, y], own_part]).astype(BF16)
    near = sum_core(0, z)
    finish(flight)
    flight = share_core(far)
    finish(near)
    add_core(0, z)
    near = sum_plane(0)
    finish(flight)
    attend(far)
    flight = sum_core(1, far)
    finish(near)
    add_plane(0)
    finish(flight)
    add_core(1, far)
    finish(sum_plane(1))
    add_plane(1)
    flight = [start(s3.at[1], rz, to_z)]
    spread = onehot(place(iota((64, 1024), 0)) == (iota((64, 1024), 1) >> 4))
    wide = dot(slot_half, spread)
    wide = jnp.where(iota((16, 1024), 0) == (iota((16, 1024), 1) & 3), wide, 0.0)
    wide = jnp.sum(wide, axis=0, keepdims=True)
    lane = iota((1, 1024), 1)
    code = jnp.where(wide < -0.5, -1.0, wide + MOSTE * ((lane >> 2) & 3).astype(F32))
    choose[...] = onehot(iota((4 * MOSTE, 1024), 0) == code.astype(jnp.int32))
    spread = onehot(place(iota((64, 256), 0)) == (iota((64, 256), 1) >> 2))
    wide = dot(slot_half, spread)
    wide = jnp.where(iota((16, 256), 0) == (iota((16, 256), 1) & 3), wide, 0.0)
    wide = jnp.sum(wide, axis=0, keepdims=True).astype(jnp.int32)
    back = onehot(iota((MOSTE, 256), 0) == wide)
    slot_weight = jnp.zeros((MOSTE, 1), F32)
    slot_whole = slot.astype(jnp.int32)
    for t in range(4):
        mine = iota((MOSTE, 64), 0) == slot_whole[t:t + 1]
        slot_weight = slot_weight + jnp.sum(
            jnp.where(mine, weights[t], 0.0), axis=1, keepdims=True
        )
    finish(flight)
    final = merge([s3[0], rz[...]])
    lane = iota((16, 128), 1)
    attended = jnp.where(lane >= HEAD, final / (final[:, 1:2] + final[:, 2:3]), 0.0).astype(BF16)

    row, col = iota((128, 256), 0), iota((128, 256), 1)
    copies = onehot((row >= HEAD) & ((col & (HEAD - 1)) == row - HEAD))
    heads = jnp.where(own_head, dot(attended, copies), 0.0)
    steps = onehot((iota((16, 16), 1) & 3) == iota((16, 16), 0))
    attended = dot(steps, heads.astype(BF16)).astype(BF16)
    proj[:, PADDED - 128:] = jnp.zeros((8, 128), F32)
    loads[2].wait()
    proj[:, :D] = dot(attended, wout_ref[...], ((1,), (1,)))[0:8]
    for k in range(KV):
        rsend[k] = window(proj, k)[0:4].astype(BF16)
    finish([
        start(rsend.at[peer], rrecv.at[k], to_kv[k]) for k, peer in enumerate(peers)
    ])
    projected = rsend[kv].astype(F32)
    for d in range(KV - 1):
        projected = projected + rrecv[d].astype(F32)
    lane = iota((4, LANES), 1)
    residual_sum = jnp.where(lane < SLICE, padr[0:4, :] + projected, 0.0)

    squares = jnp.sum(residual_sum * residual_sum, axis=1, keepdims=True)
    high = squares.astype(BF16).astype(F32)
    scaled = residual_sum * padg[...]
    agbuf[column] = jnp.where(
        lane == SLICE, high, jnp.where(lane == SLICE + 1, squares - high, scaled)
    ).astype(BF16)
    finish([start(agbuf.at[column], agbuf.at[column], device) for device in to_column])
    for zz in range(NZ):
        pieces = [agbuf[KV * zz + k].astype(F32) for k in range(KV)]
        squares = jnp.zeros((4, 1), F32)
        for piece in pieces:
            squares = squares + piece[:, SLICE:SLICE + 1] + piece[:, SLICE + 1:SLICE + 2]
        inverse = lax.rsqrt(squares / D + 1e-05)
        high = inverse.astype(BF16).astype(F32)
        for k, piece in enumerate(pieces):
            piece = jnp.where(
                lane == SLICE, high, jnp.where(lane == SLICE + 1, inverse - high, piece)
            )
            low, half = 16 * zz + 4 * (k // 2), LANES * (k % 2)
            blk[low:low + 4, half:half + LANES] = piece
    block = blk[...]
    block = jnp.where(
        iota(block.shape, 1) < SLICE, block, pltpu.roll(block, WIDE - (LANES - SLICE), 1)
    ).astype(BF16)
    ybuf[0, c, x, y] = block[0:16]
    ybuf[1, c, x, y] = block[16:32]

    a = [start(ybuf.at[0, c, x, y], ybuf.at[0, c, x, y], device) for device in to_y]
    b = [start(ybuf.at[1, c, x, y], ybuf.at[1, c, x, y], device) for device in to_x]
    finish(a)
    a = [start(ybuf.at[0, c, x], ybuf.at[0, c, x], device) for device in to_x]
    cores = [start(ybuf.at[0, c, x], ybuf.at[0, c, x], to_core)]
    finish(b)
    b = [start(ybuf.at[1, c, :, y], ybuf.at[1, c, :, y], device) for device in to_y]
    cores.append(start(ybuf.at[1, c, :, y], ybuf.at[1, c, :, y], to_core))
    for d in (1, 3, 2):
        a[d - 1].wait()
        xx = lax.rem(x + NX - d, NX)
        cores.append(start(ybuf.at[0, c, xx], ybuf.at[0, c, xx], to_core))
        b[d - 1].wait()
        yy = lax.rem(y + NY - d, NY)
        cores.append(start(ybuf.at[1, c, :, yy], ybuf.at[1, c, :, yy], to_core))
    for load in loads[3:]:
        load.wait()
    finish(cores)

    rows = dot(choose[...], ybuf[...].reshape(1024, WIDE))
    factor = rows[0:MOSTE, QUARTER:QUARTER + 1] + rows[0:MOSTE, QUARTER + 1:QUARTER + 2]
    xs[...] = jnp.zeros(xs.shape, F32)
    for j in range(4):
        low = QUARTER * j // 128 * 128
        features = jnp.where(
            iota((MOSTE, WIDE), 1) < QUARTER, rows[MOSTE * j:MOSTE * (j + 1)], 0.0
        )
        features = jnp.concatenate([features, jnp.zeros((MOSTE, 128), F32)], axis=1)
        if QUARTER * j - low:
            features = pltpu.roll(features, QUARTER * j - low, 1)
        xs[:, low:low + WIDE + 128] += features
    features = xs[:, :D].astype(BF16)
    gate = dot(features, wg_ref[...], ((1,), (1,))) * factor
    up = dot(features, wu_ref[...], ((1,), (1,))) * factor
    activation = (gate * jax.nn.sigmoid(1.702 * gate) * (up + 1.0)).astype(BF16)
    oflat[:, PADDED - 128:] = jnp.zeros((MOSTE, 128), F32)
    oflat[:, :D] = dot(activation, wd_ref[...]) * slot_weight
    for k in range(KV):
        esend[k] = window(oflat, k).astype(BF16)
    finish([
        start(esend.at[peer], erecv.at[k], to_kv[k]) for k, peer in enumerate(peers)
    ])
    summed = esend[kv].astype(F32)
    for d in range(KV - 1):
        summed = summed + erecv[d].astype(F32)

    dense = dot(back, summed.astype(BF16), ((0,), (0,)))
    dn[...] = dense.astype(BF16).reshape(dn.shape)

    def fold_half(i, h):
        finish([start(dn.at[h, 1 - c], r1.at[i], to_core)])
        total = dn[h, c].astype(F32) + r1[i].astype(F32)
        for xx in range(NX):
            for yy in range(NY):
                low = 4 * (NY * xx + yy)
                e1[i, xx, yy] = total[low:low + 4].astype(BF16)
        finish([
            start(e1.at[i, xx, yy], rx2.at[i, k], to_plane[k])
            for k, (xx, yy) in enumerate(in_plane)
        ])
        total = e1[i, x, y].astype(F32)
        for k in range(len(others)):
            total = total + rx2[i, k].astype(F32)
        e3[i] = total

    fold_half(1, far)
    across = [start(e3.at[1], rz2, to_z)]
    fold_half(0, z)
    finish(across)
    out = residual_sum + e3[0] + rz2[...]
    out_ref[...] = out[:, 0:SLICE].astype(BF16)


def on_device(
    queries, prompt_cache, gen_cache, gen_lengths, new_kv, w_out, residual, norm_gain,
    w_gate, w_up, w_down, expert_ids, route_weights,
):
    ffe = w_gate.shape[2]
    anywhere = pl.BlockSpec(memory_space=pl.ANY)
    vmem = pl.BlockSpec(memory_space=pltpu.VMEM)
    smem = pl.BlockSpec(memory_space=pltpu.SMEM)
    grid = (NZ, NC, NX, NY)
    scratch = [
        pltpu.VMEM(prompt_cache.shape, BF16),
        pltpu.VMEM(gen_cache.shape[1:], BF16),
        pltpu.VMEM((D, 256), BF16),
        pltpu.VMEM((ffe, D), BF16),
        pltpu.VMEM((ffe, D), BF16),
        pltpu.VMEM((ffe, D), BF16),
        pltpu.VMEM((16, 256), F32),
        pltpu.VMEM((16, 128), F32),
        pltpu.VMEM((8, LANES), F32),
        pltpu.VMEM((1, LANES), F32),
        pltpu.VMEM((16, 64), F32),
        pltpu.VMEM(grid + (16, 128), BF16),
        pltpu.VMEM(grid + (16, 128), BF16),
        pltpu.VMEM((2, NX, NY, 16, 128), BF16),
        pltpu.VMEM((2, NX, NY, 16, 128), BF16),
        pltpu.VMEM((2, NX * NY - 1, 16, 128), BF16),
        pltpu.VMEM((2, 16, 128), F32),
        pltpu.VMEM((16, 128), F32),
        pltpu.VMEM((8, PADDED), F32),
        pltpu.VMEM((KV, 4, LANES), BF16),
        pltpu.VMEM((KV - 1, 4, LANES), BF16),
        pltpu.VMEM((NZ * KV, 4, LANES), BF16),
        pltpu.VMEM((32, WIDE), F32),
        pltpu.VMEM(grid + (16, WIDE), BF16),
        pltpu.VMEM((4 * MOSTE, 1024), BF16),
        pltpu.VMEM((MOSTE, PADDED), F32),
        pltpu.VMEM((MOSTE, PADDED), F32),
        pltpu.VMEM((KV, MOSTE, LANES), BF16),
        pltpu.VMEM((KV - 1, MOSTE, LANES), BF16),
        pltpu.VMEM((NZ, NC, 64, LANES), BF16),
        pltpu.VMEM((2, 64, LANES), BF16),
        pltpu.VMEM((2, NX, NY, 4, LANES), BF16),
        pltpu.VMEM((2, NX * NY - 1, 4, LANES), BF16),
        pltpu.VMEM((2, 4, LANES), F32),
        pltpu.VMEM((4, LANES), F32),
        pltpu.SemaphoreType.DMA((160,)),
        pltpu.SemaphoreType.DMA((160,)),
        pltpu.SemaphoreType.DMA((6,)),
    ]
    out = pl.pallas_call(
        kernel,
        out_shape=jax.ShapeDtypeStruct(residual.shape[1:], BF16),
        in_specs=[vmem, anywhere, anywhere, vmem, smem, anywhere, vmem, vmem]
        + [anywhere] * 3 + [vmem] * 2,
        out_specs=vmem,
        scratch_shapes=scratch,
        compiler_params=pltpu.CompilerParams(
            collective_id=0, has_side_effects=True, vmem_limit_bytes=60 * 1024 * 1024
        ),
        name="layer",
    )(
        queries[0], prompt_cache, gen_cache[0], new_kv[0], gen_lengths, w_out.T, residual[0],
        norm_gain, w_gate[0].T, w_up[0].T, w_down[0],
        expert_ids.transpose(1, 2, 0), route_weights.transpose(1, 2, 0),
    )
    return out[None]


def solution(mesh):
    in_specs = (
        P("roll", None, "kv"),
        P(None, "roll", "kv"),
        P("roll", None, "kv"),
        P("roll"),
        P("roll", None, "kv"),
        P("kv", None),
        P("roll", None, "kv"),
        P("kv"),
        P("roll", None, "kv"),
        P("roll", None, "kv"),
        P("roll", "kv", None),
        P(),
        P(),
    )
    out_specs = P("roll", None, "kv")
    return jax.shard_map(
        on_device, mesh=mesh, in_specs=in_specs, out_specs=out_specs, check_vma=False
    )
```
